32 devices in a mesh: tm: 4 (over z), gx: 2 (over x), gy: 4 (over y, core).
Axes of the slice: x: 2, y: 2, z: 4, core: 2. Of those that a mesh axis runs over, the one named last changes fastest.
Arguments:
- state_starts: float32 [4, 64, 64, 512], P('tm', None, 'gx', 'gy'), may hold values from -4 to 4, as said below
- diffusivity: float32 [64], replicated, may hold values from 0.3 to 1.2
- wind: float32 [2, 64], replicated, may hold values from -0.6 to 0.6
Outputs:
- segment_ends: float32 [4, 64, 64, 512], P('tm', None, 'gx', 'gy')
The draws below stay inside these ranges and needn't reach their ends.
Inputs may be any that keep to these rules, and one draw needn't show every extreme that they name: `state_starts`: states of order one.
All inputs are finite; a program needn't handle non-finite values.
Results may differ from the reference program's by a relative error of at most 0.0001.
Values sent between devices are 32-bit elements; how exact they have to be, the bound alone decides.
A program may use at most 64 MiB of HBM per device.

```python
import math
import jax
import jax.numpy as jnp

L = 64
SUB = 4
SEGMENTS = 4
NX = 64
NY = 512


def draw_state_starts(key, part):
    shape = (SEGMENTS, L, NX, NY)
    return jnp.clip(jax.random.normal(key, shape, jnp.float32), -4.0, 4.0)


def setup_inputs(seed: int = 0) -> dict:
    arg_keys = jax.random.split(jax.random.key(seed), 4)
    return {
        "state_starts": draw_state_starts(jax.random.fold_in(arg_keys[3], 71), 0),
        "diffusivity": jnp.clip(jnp.exp(jax.random.uniform(arg_keys[1], (L,), jnp.float32, math.log(0.3), math.log(1.2))), 0.3, 1.2),
        "wind": jnp.clip(jax.random.uniform(arg_keys[2], (2, L), jnp.float32, -0.6, 0.6), -0.6, 0.6),
    }


time_step = 0.2
weights_low = (0.375, 0.125, 0.0, 0.0)
weights_mid = (0.625, 0.875, 0.875, 0.625)
weights_high = (0.0, 0.0, 0.125, 0.375)


def advance(padded, diffuse, wind_east, wind_north, factor):
    centre = padded[:, 1:-1, 1:-1]
    east = padded[:, 2:, 1:-1]
    west = padded[:, :-2, 1:-1]
    north = padded[:, 1:-1, 2:]
    south = padded[:, 1:-1, :-2]
    laplace = east + west + north + south - 4.0 * centre
    slope = wind_east * (east - west) * 0.5 + wind_north * (north - south) * 0.5
    return centre + time_step * (factor * diffuse * laplace - centre * slope)


def pad_zero(field):
    return jnp.pad(field, ((0, 0), (1, 1), (1, 1)))


def restrict(field):
    levels, rows, cols = field.shape
    return field.reshape(levels, rows // 4, 4, cols // 4, 4).mean(axis=(2, 4))


def prolong(padded):
    levels, rows_ext, cols_ext = padded.shape
    coarse_rows = rows_ext - 2
    coarse_cols = cols_ext - 2
    parts = [weights_low[offset] * padded[:, :-2, :] + weights_mid[offset] * padded[:, 1:-1, :] + weights_high[offset] * padded[:, 2:, :] for offset in range(4)]
    along = jnp.stack(parts, axis=2).reshape(levels, 4 * coarse_rows, cols_ext)
    parts = [weights_low[offset] * along[:, :, :-2] + weights_mid[offset] * along[:, :, 1:-1] + weights_high[offset] * along[:, :, 2:] for offset in range(4)]
    return jnp.stack(parts, axis=3).reshape(levels, 4 * coarse_rows, 4 * coarse_cols)


def reference(state_starts, diffusivity, wind):
    diffuse = diffusivity[:, None, None]
    wind_east = wind[0][:, None, None]
    wind_north = wind[1][:, None, None]
    fine_ends = []
    old_images = []
    coarse_first = restrict(state_starts[0])
    for segment in range(SEGMENTS):
        field = state_starts[segment]
        for substep in range(SUB):
            field = advance(pad_zero(field), diffuse, wind_east, wind_north, 1.0)
        fine_ends.append(field)
        coarse_old = restrict(state_starts[segment])
        old_images.append(advance(pad_zero(coarse_old), diffuse, wind_east, wind_north, 0.25))
    coarse = coarse_first
    results = []
    for segment in range(SEGMENTS):
        change = advance(pad_zero(coarse), diffuse, wind_east, wind_north, 0.25) - old_images[segment]
        ending = fine_ends[segment] + prolong(pad_zero(change))
        results.append(ending)
        coarse = restrict(ending)
    return jnp.stack(results)
```

```python
import functools

import jax
import jax.numpy as jnp
from jax import lax
from jax.experimental import pallas as pl
from jax.experimental.pallas import tpu as pltpu
from jax.sharding import PartitionSpec as P

SUB = 4
REACH = SUB
RATIO = 4
LANES = 128
EDGE = 8
FRONT = 2 * EDGE
COARSE_REACH = 2

time_step = 0.2
weights_low = (0.375, 0.125, 0.0, 0.0)
weights_mid = (0.625, 0.875, 0.875, 0.625)
weights_high = (0.0, 0.0, 0.125, 0.375)
mean_side, mean_mid = 0.125, 0.75

PLANE = tuple((dx, dy) for dx in (-1, 0, 1) for dy in (-1, 0, 1))
AROUND = tuple(d for d in PLANE if d != (0, 0))


def conjunction(conditions):
    total = True
    for condition in conditions:
        total = condition if total is True else jnp.logical_and(total, condition)
    return total


def kernel(
    sizes, levels, rows, cols,
    x_ref, diff_ref, wind_ref, out_ref,
    first, second, x_send, x_recv, old_wide, new_wide, extended, old_image, change,
    sent, fine_mean, line, fine_line,
    fine_out, fine_in, old_out, old_in, chain_out, chain_in,
):
    n_tm, n_gx, n_gy = sizes
    tm, gx, gy = lax.axis_index("tm"), lax.axis_index("gx"), lax.axis_index("gy")
    packs = LANES // levels
    part = rows // packs
    part_c = part // RATIO
    cols_c = cols // RATIO
    wide = part + 2 * REACH
    wide_c = part_c + 2 * COARSE_REACH
    end = FRONT + cols
    end_c = FRONT + cols_c

    def there(dz, dx, dy):
        tests = []
        for place, move, count in ((tm, dz, n_tm), (gx, dx, n_gx), (gy, dy, n_gy)):
            if move < 0:
                tests.append(place > 0)
            if move > 0:
                tests.append(place < count - 1)
        return conjunction(tests)

    def guarded(condition, action):
        if condition is True:
            action()
        else:
            pl.when(condition)(action)

    def target(dz, dx, dy):
        return (tm + dz, gx + dx, gy + dy)

    barrier = pltpu.get_barrier_semaphore()
    partners = [(dz, dx, dy) for dz in (-1, 0, 1) for dx, dy in PLANE if (dz, dx, dy) != (0, 0, 0)]
    awaited = jnp.int32(0)
    for move in partners:
        def greet(move=move):
            pl.semaphore_signal(barrier, inc=1, device_id=target(*move), device_id_type=pl.DeviceIdType.MESH)
        guarded(there(*move), greet)
        awaited = awaited + there(*move).astype(jnp.int32)

    def send_all(copies, dz, moves):
        for move in moves:
            guarded(there(dz, *move), lambda move=move: copies[move].start())

    def sends_done(copies, dz, moves):
        for move in moves:
            guarded(there(dz, *move), lambda move=move: copies[move].wait_send())

    def all_arrived(copies, dz, moves):
        for dx, dy in moves:
            guarded(there(-dz, -dx, -dy), lambda move=(dx, dy): copies[move].wait_recv())

    def remote(source, landing, out_sem, in_sem, move):
        return pltpu.make_async_remote_copy(
            src_ref=source, dst_ref=landing, send_sem=out_sem, recv_sem=in_sem,
            device_id=target(*move), device_id_type=pl.DeviceIdType.MESH,
        )

    def index_of(move):
        return (move[0] + 1) * 3 + move[1] + 1

    fine_copies = {}
    for move in AROUND:
        dx, dy = move
        k = index_of(move)
        if dy == 0:
            source, landing = x_send.at[(dx + 1) // 2], x_recv.at[(dx + 1) // 2]
        else:
            take_row, put_row, height = {
                0: (REACH, REACH, part), -1: (REACH, REACH + part, REACH), 1: (part, 0, REACH)
            }[dx]
            take, put = {-1: (FRONT, end), 1: (end - EDGE, FRONT - EDGE)}[dy]
            source = first.at[pl.ds(take_row, height), pl.ds(take, EDGE)]
            landing = first.at[pl.ds(put_row, height), pl.ds(put, EDGE)]
        fine_copies[move] = remote(source, landing, fine_out.at[k], fine_in.at[k], (0, dx, dy))

    def coarse_copies(buffer, row0, col0, landing_buffer, out_sems, in_sems, dz, moves):
        copies = {}
        for move in moves:
            dx, dy = move
            k = index_of(move)
            take_row, put_row, height = {
                0: (0, COARSE_REACH, part_c),
                -1: (0, COARSE_REACH + part_c, COARSE_REACH),
                1: (part_c - COARSE_REACH, 0, COARSE_REACH),
            }[dx]
            take, put, width = {
                0: (0, FRONT, cols_c), -1: (0, end_c, EDGE), 1: (cols_c - EDGE, FRONT - EDGE, EDGE)
            }[dy]
            copies[move] = remote(
                buffer.at[pl.ds(row0 + take_row, height), pl.ds(col0 + take, width)],
                landing_buffer.at[pl.ds(put_row, height), pl.ds(put, width)],
                out_sems.at[k], in_sems.at[k], (dz, dx, dy),
            )
        return copies

    old_copies = coarse_copies(old_wide, COARSE_REACH, FRONT, old_wide, old_out, old_in, 0, AROUND)
    chain_copies = coarse_copies(sent, 0, 0, new_wide, chain_out, chain_in, 1, PLANE)

    lane = lax.broadcasted_iota(jnp.int32, (1, LANES), 1)
    pack = lane // levels

    def packed(row):
        return jnp.concatenate([row] * packs, axis=1)

    diffuse = packed(diff_ref[...])
    east_wind = packed(wind_ref[0:1, :])
    north_wind = packed(wind_ref[1:2, :])

    def constants(factor):
        spread = (time_step * factor) * diffuse
        return 1.0 - 4.0 * spread, spread, (0.5 * time_step) * east_wind, (0.5 * time_step) * north_wind

    fine_constants = constants(1.0)
    coarse_constants = constants(0.25)

    def advance(source, row, start, count, consts):
        keep, spread, along_x, along_y = consts
        centre = source[row, pl.ds(start, count), :]
        east = source[row + 1, pl.ds(start, count), :]
        west = source[row - 1, pl.ds(start, count), :]
        north = source[row, pl.ds(start + 1, count), :]
        south = source[row, pl.ds(start - 1, count), :]
        pushed = along_x * (east - west) + along_y * (north - south)
        return centre * (keep - pushed) + spread * ((east + west) + (north + south))

    def native_row(x):
        if x < 0:
            return x_recv[1, x + REACH]
        if x >= rows:
            return x_recv[0, x - rows]
        return x_ref[pl.ds(x, levels, stride=rows), :]

    def bring_in(row):
        stacked = jnp.concatenate([native_row(p * part + row - REACH) for p in range(packs)], axis=0)
        first[row, pl.ds(FRONT, cols), :] = stacked.T

    for r in range(REACH):
        x_send[0, r] = native_row(r)
        x_send[1, r] = native_row(rows - REACH + r)
    pl.semaphore_wait(barrier, awaited)
    x_moves = tuple(m for m in AROUND if m[1] == 0)
    y_moves = tuple(m for m in AROUND if m[1] != 0)
    send_all(fine_copies, 0, x_moves)
    for row in range(REACH, REACH + part):
        bring_in(row)
    send_all(fine_copies, 0, y_moves)

    def restricted(source, row):
        total = source[REACH + row * RATIO, pl.ds(FRONT, cols), :]
        for r in range(1, RATIO):
            total = total + source[REACH + row * RATIO + r, pl.ds(FRONT, cols), :]
        fine_line[...] = total
        mean = fine_line[pl.ds(0, cols_c, stride=RATIO), :]
        for o in range(1, RATIO):
            mean = mean + fine_line[pl.ds(o, cols_c, stride=RATIO), :]
        return mean * (1.0 / RATIO**2)

    for row in range(part_c):
        old_wide[COARSE_REACH + row, pl.ds(FRONT, cols_c), :] = restricted(first, row)
    send_all(old_copies, 0, AROUND)

    def inside_x(row, reach, length):
        place = (gx * packs + pack) * length + (row - reach)
        return jnp.logical_and(place >= 0, place < n_gx * packs * length)

    def inside_y(start, count, length):
        place = gy * length + (start - FRONT) + lax.broadcasted_iota(jnp.int32, (count, LANES), 0)
        return jnp.logical_and(place >= 0, place < n_gy * length)

    all_arrived(fine_copies, 0, x_moves)
    for row in [*range(REACH), *range(REACH + part, wide)]:
        bring_in(row)
        inner = first[row, pl.ds(FRONT, cols), :]
        first[row, pl.ds(FRONT, cols), :] = jnp.where(inside_x(row, REACH, part), inner, 0.0)
    all_arrived(fine_copies, 0, y_moves)
    sends_done(fine_copies, 0, AROUND)
    low_lanes = lane < levels
    high_lanes = lane >= LANES - levels
    for start in (FRONT - EDGE, end):
        mask_y = inside_y(start, EDGE, cols)
        for row in [*range(REACH), *range(REACH + part, wide), *range(REACH, REACH + part)]:
            here = first[row, pl.ds(start, EDGE), :]
            if row < REACH:
                here = pltpu.roll(jnp.where(high_lanes, here, first[row + part, pl.ds(start, EDGE), :]), levels, 1)
            elif row >= REACH + part:
                here = pltpu.roll(jnp.where(low_lanes, here, first[row - part, pl.ds(start, EDGE), :]), LANES - levels, 1)
            mask = mask_y
            if not REACH <= row < REACH + part:
                mask = jnp.logical_and(mask, inside_x(row, REACH, part))
            first[row, pl.ds(start, EDGE), :] = jnp.where(mask, here, 0.0)

    south_mask = inside_y(FRONT - EDGE, EDGE, cols)
    north_mask = inside_y(end, EDGE, cols)
    half = cols // 2
    source, dest = first, second
    for step in range(1, SUB + 1):
        def one_row(row, source=source, dest=dest, last=step == SUB):
            mask_x = inside_x(row, REACH, part)
            pieces = [(FRONT, half, None), (FRONT + half, cols - half, None)]
            if not last:
                pieces += [(FRONT - EDGE, EDGE, south_mask), (end, EDGE, north_mask)]
            for start, count, mask_y in pieces:
                value = advance(source, row, start, count, fine_constants)
                mask = mask_x if mask_y is None else jnp.logical_and(mask_x, mask_y)
                if not (last and mask_y is None):
                    value = jnp.where(mask, value, 0.0)
                dest[row, pl.ds(start, count), :] = value

        pl.loop(step, wide - step)(one_row)
        source, dest = dest, source
    fine = source

    for row in range(part_c):
        fine_mean[row] = restricted(fine, row)

    count_c = cols_c + 2 * EDGE
    begin_c = FRONT - EDGE
    mask_y = inside_y(begin_c, count_c, cols_c)

    def extend(buffer):
        for row in range(wide_c):
            here = buffer[row, pl.ds(begin_c, count_c), :]
            if row < COARSE_REACH:
                here = pltpu.roll(
                    jnp.where(high_lanes, here, buffer[row + part_c, pl.ds(begin_c, count_c), :]), levels, 1
                )
            elif row >= COARSE_REACH + part_c:
                here = pltpu.roll(
                    jnp.where(low_lanes, here, buffer[row - part_c, pl.ds(begin_c, count_c), :]), LANES - levels, 1
                )
            mask = jnp.logical_and(mask_y, inside_x(row, COARSE_REACH, part_c))
            extended[row, pl.ds(begin_c, count_c), :] = jnp.where(mask, here, 0.0)

    all_arrived(old_copies, 0, AROUND)
    sends_done(old_copies, 0, AROUND)
    extend(old_wide)
    for row in range(1, wide_c - 1):
        old_image[row - 1] = advance(extended, row, begin_c, count_c, coarse_constants)

    @pl.when(tm > 0)
    def _():
        all_arrived(chain_copies, 1, PLANE)
        extend(new_wide)

    for row in range(1, wide_c - 1):
        moved = advance(extended, row, begin_c, count_c, coarse_constants) - old_image[row - 1]
        mask = jnp.logical_and(mask_y, inside_x(row, COARSE_REACH, part_c))
        change[row - 1, pl.ds(begin_c, count_c), :] = jnp.where(mask, moved, 0.0)

    def change_row(row):
        return change[row, pl.ds(begin_c, count_c), :]

    @pl.when(tm < n_tm - 1)
    def _():
        for row in range(part_c):
            line[pl.ds(begin_c, count_c), :] = (
                mean_side * (change_row(row) + change_row(row + 2)) + mean_mid * change_row(row + 1)
            )
            sides = line[pl.ds(FRONT - 1, cols_c), :] + line[pl.ds(FRONT + 1, cols_c), :]
            sent[row] = fine_mean[row] + mean_side * sides + mean_mid * line[pl.ds(FRONT, cols_c), :]
        send_all(chain_copies, 1, PLANE)

    def blend(offset, low, mid, high):
        total = weights_mid[offset] * mid
        if weights_low[offset]:
            total = total + weights_low[offset] * low
        if weights_high[offset]:
            total = total + weights_high[offset] * high
        return total

    for row in range(part):
        at, offset = row // RATIO, row % RATIO
        line[pl.ds(begin_c, count_c), :] = blend(offset, change_row(at), change_row(at + 1), change_row(at + 2))
        low, mid, high = (line[pl.ds(FRONT + d, cols_c), :] for d in (-1, 0, 1))
        for o in range(RATIO):
            fine_line[pl.ds(o, cols_c, stride=RATIO), :] = blend(o, low, mid, high)
        ending = (fine[REACH + row, pl.ds(FRONT, cols), :] + fine_line[...]).T
        for p in range(packs):
            out_ref[pl.ds(p * part + row, levels, stride=rows), :] = ending[p * levels : (p + 1) * levels]

    pl.when(tm < n_tm - 1)(lambda: sends_done(chain_copies, 1, PLANE))


def shards(sizes, state_starts, diffusivity, wind):
    _, levels, rows, cols = state_starts.shape
    packs = LANES // levels
    part = rows // packs
    part_c = part // RATIO
    cols_c = cols // RATIO
    wide, wide_c = part + 2 * REACH, part_c + 2 * COARSE_REACH
    vmem = functools.partial(pltpu.VMEM, dtype=jnp.float32)
    scratch = [
        vmem((wide, cols + 2 * FRONT, LANES)),
        vmem((wide, cols + 2 * FRONT, LANES)),
        vmem((2, REACH, levels, cols)),
        vmem((2, REACH, levels, cols)),
        vmem((wide_c, cols_c + 2 * FRONT, LANES)),
        vmem((wide_c, cols_c + 2 * FRONT, LANES)),
        vmem((wide_c, cols_c + 2 * FRONT, LANES)),
        vmem((wide_c - 2, cols_c + 2 * EDGE, LANES)),
        vmem((wide_c - 2, cols_c + 2 * FRONT, LANES)),
        vmem((part_c, cols_c, LANES)),
        vmem((part_c, cols_c, LANES)),
        vmem((cols_c + 2 * FRONT, LANES)),
        vmem((cols, LANES)),
    ] + [pltpu.SemaphoreType.DMA((9,))] * 6
    in_vmem = pl.BlockSpec(memory_space=pltpu.VMEM)
    ending = pl.pallas_call(
        functools.partial(kernel, sizes, levels, rows, cols),
        out_shape=jax.ShapeDtypeStruct((levels * rows, cols), jnp.float32),
        in_specs=[in_vmem] * 3,
        out_specs=in_vmem,
        scratch_shapes=scratch,
        compiler_params=pltpu.CompilerParams(collective_id=0, has_side_effects=True),
        name="parareal",
    )(state_starts.reshape(levels * rows, cols), diffusivity.reshape(1, levels), wind)
    return ending.reshape(1, levels, rows, cols)


def solution(mesh):
    sizes = tuple(mesh.shape[axis] for axis in ("tm", "gx", "gy"))
    placed = (P("tm", None, "gx", "gy"), P(), P())
    return jax.shard_map(
        functools.partial(shards, sizes),
        mesh=mesh, in_specs=placed, out_specs=P("tm", None, "gx", "gy"), check_vma=False,
    )
```

```python
import functools

import jax
import jax.numpy as jnp
from jax import lax
from jax.experimental import pallas as pl
from jax.experimental.pallas import tpu as pltpu
from jax.sharding import PartitionSpec as P

SUB = 4
REACH = SUB
RATIO = 4
LANES = 128
EDGE = 8
FRONT = 2 * EDGE
COARSE_REACH = 2

time_step = 0.2
weights_low = (0.375, 0.125, 0.0, 0.0)
weights_mid = (0.625, 0.875, 0.875, 0.625)
weights_high = (0.0, 0.0, 0.125, 0.375)
mean_side, mean_mid = 0.125, 0.75

PLANE = tuple((dx, dy) for dx in (-1, 0, 1) for dy in (-1, 0, 1))
AROUND = tuple(d for d in PLANE if d != (0, 0))


def conjunction(conditions):
    total = True
    for condition in conditions:
        total = condition if total is True else jnp.logical_and(total, condition)
    return total


def kernel(
    sizes, levels, rows, cols,
    x_ref, diff_ref, wind_ref, out_ref,
    first, second, x_send, x_recv, old_wide, new_wide, extended, old_image, change,
    sent, fine_mean, line, fine_line,
    fine_out, fine_in, old_out, old_in, chain_out, chain_in,
):
    n_tm, n_gx, n_gy = sizes
    tm, gx, gy = lax.axis_index("tm"), lax.axis_index("gx"), lax.axis_index("gy")
    packs = LANES // levels
    part = rows // packs
    part_c = part // RATIO
    cols_c = cols // RATIO
    wide = part + 2 * REACH
    wide_c = part_c + 2 * COARSE_REACH
    end = FRONT + cols
    end_c = FRONT + cols_c

    def there(dz, dx, dy):
        tests = []
        for place, move, count in ((tm, dz, n_tm), (gx, dx, n_gx), (gy, dy, n_gy)):
            if move < 0:
                tests.append(place > 0)
            if move > 0:
                tests.append(place < count - 1)
        return conjunction(tests)

    def guarded(condition, action):
        if condition is True:
            action()
        else:
            pl.when(condition)(action)

    def target(dz, dx, dy):
        return (tm + dz, gx + dx, gy + dy)

    barrier = pltpu.get_barrier_semaphore()
    partners = [(dz, dx, dy) for dz in (-1, 0, 1) for dx, dy in PLANE if (dz, dx, dy) != (0, 0, 0)]
    awaited = jnp.int32(0)
    for move in partners:
        def greet(move=move):
            pl.semaphore_signal(barrier, inc=1, device_id=target(*move), device_id_type=pl.DeviceIdType.MESH)
        guarded(there(*move), greet)
        awaited = awaited + there(*move).astype(jnp.int32)

    def send_all(copies, dz, moves):
        for move in moves:
            guarded(there(dz, *move), lambda move=move: copies[move].start())

    def sends_done(copies, dz, moves):
        for move in moves:
            guarded(there(dz, *move), lambda move=move: copies[move].wait_send())

    def all_arrived(copies, dz, moves):
        for dx, dy in moves:
            guarded(there(-dz, -dx, -dy), lambda move=(dx, dy): copies[move].wait_recv())

    def remote(source, landing, out_sem, in_sem, move):
        return pltpu.make_async_remote_copy(
            src_ref=source, dst_ref=landing, send_sem=out_sem, recv_sem=in_sem,
            device_id=target(*move), device_id_type=pl.DeviceIdType.MESH,
        )

    def index_of(move):
        return (move[0] + 1) * 3 + move[1] + 1

    fine_copies = {}
    for move in AROUND:
        dx, dy = move
        k = index_of(move)
        if dy == 0:
            source, landing = x_send.at[(dx + 1) // 2], x_recv.at[(dx + 1) // 2]
        else:
            take_row, put_row, height = {
                0: (REACH, REACH, part), -1: (REACH, REACH + part, REACH), 1: (part, 0, REACH)
            }[dx]
            take, put = {-1: (FRONT, end), 1: (end - EDGE, FRONT - EDGE)}[dy]
            source = first.at[pl.ds(take_row, height), pl.ds(take, EDGE)]
            landing = first.at[pl.ds(put_row, height), pl.ds(put, EDGE)]
        fine_copies[move] = remote(source, landing, fine_out.at[k], fine_in.at[k], (0, dx, dy))

    def coarse_copies(buffer, row0, col0, landing_buffer, out_sems, in_sems, dz, moves):
        copies = {}
        for move in moves:
            dx, dy = move
            k = index_of(move)
            take_row, put_row, height = {
                0: (0, COARSE_REACH, part_c),
                -1: (0, COARSE_REACH + part_c, COARSE_REACH),
                1: (part_c - COARSE_REACH, 0, COARSE_REACH),
            }[dx]
            take, put, width = {
                0: (0, FRONT, cols_c), -1: (0, end_c, EDGE), 1: (cols_c - EDGE, FRONT - EDGE, EDGE)
            }[dy]
            copies[move] = remote(
                buffer.at[pl.ds(row0 + take_row, height), pl.ds(col0 + take, width)],
                landing_buffer.at[pl.ds(put_row, height), pl.ds(put, width)],
                out_sems.at[k], in_sems.at[k], (dz, dx, dy),
            )
        return copies

    old_copies = coarse_copies(old_wide, COARSE_REACH, FRONT, old_wide, old_out, old_in, 0, AROUND)
    chain_copies = coarse_copies(sent, 0, 0, new_wide, chain_out, chain_in, 1, PLANE)

    lane = lax.broadcasted_iota(jnp.int32, (1, LANES), 1)
    pack = lane // levels

    def packed(row):
        return jnp.concatenate([row] * packs, axis=1)

    diffuse = packed(diff_ref[...])
    east_wind = packed(wind_ref[0:1, :])
    north_wind = packed(wind_ref[1:2, :])

    def constants(factor):
        spread = (time_step * factor) * diffuse
        return 1.0 - 4.0 * spread, spread, (0.5 * time_step) * east_wind, (0.5 * time_step) * north_wind

    fine_constants = constants(1.0)
    coarse_constants = constants(0.25)

    def advance(source, row, start, count, consts):
        keep, spread, along_x, along_y = consts
        centre = source[row, pl.ds(start, count), :]
        east = source[row + 1, pl.ds(start, count), :]
        west = source[row - 1, pl.ds(start, count), :]
        north = source[row, pl.ds(start + 1, count), :]
        south = source[row, pl.ds(start - 1, count), :]
        pushed = along_x * (east - west) + along_y * (north - south)
        return centre * (keep - pushed) + spread * ((east + west) + (north + south))

    def native_row(x):
        if x < 0:
            return x_recv[1, x + REACH]
        if x >= rows:
            return x_recv[0, x - rows]
        return x_ref[pl.ds(x, levels, stride=rows), :]

    def bring_in(row):
        stacked = jnp.concatenate([native_row(p * part + row - REACH) for p in range(packs)], axis=0)
        first[row, pl.ds(FRONT, cols), :] = stacked.T

    for r in range(REACH):
        x_send[0, r] = native_row(r)
        x_send[1, r] = native_row(rows - REACH + r)
    pl.semaphore_wait(barrier, awaited)
    x_moves = tuple(m for m in AROUND if m[1] == 0)
    y_moves = tuple(m for m in AROUND if m[1] != 0)
    send_all(fine_copies, 0, x_moves)
    for row in range(REACH, REACH + part):
        bring_in(row)
    send_all(fine_copies, 0, y_moves)

    def restricted(source, row):
        total = source[REACH + row * RATIO, pl.ds(FRONT, cols), :]
        for r in range(1, RATIO):
            total = total + source[REACH + row * RATIO + r, pl.ds(FRONT, cols), :]
        fine_line[...] = total
        mean = fine_line[pl.ds(0, cols_c, stride=RATIO), :]
        for o in range(1, RATIO):
            mean = mean + fine_line[pl.ds(o, cols_c, stride=RATIO), :]
        return mean * (1.0 / RATIO**2)

    for row in range(part_c):
        old_wide[COARSE_REACH + row, pl.ds(FRONT, cols_c), :] = restricted(first, row)
    send_all(old_copies, 0, AROUND)

    def inside_x(row, reach, length):
        place = (gx * packs + pack) * length + (row - reach)
        return jnp.logical_and(place >= 0, place < n_gx * packs * length)

    def inside_y(start, count, length):
        place = gy * length + (start - FRONT) + lax.broadcasted_iota(jnp.int32, (count, LANES), 0)
        return jnp.logical_and(place >= 0, place < n_gy * length)

    all_arrived(fine_copies, 0, x_moves)
    for row in [*range(REACH), *range(REACH + part, wide)]:
        bring_in(row)
        inner = first[row, pl.ds(FRONT, cols), :]
        first[row, pl.ds(FRONT, cols), :] = jnp.where(inside_x(row, REACH, part), inner, 0.0)
    all_arrived(fine_copies, 0, y_moves)
    sends_done(fine_copies, 0, AROUND)
    low_lanes = lane < levels
    high_lanes = lane >= LANES - levels
    for start in (FRONT - EDGE, end):
        mask_y = inside_y(start, EDGE, cols)
        for row in [*range(REACH), *range(REACH + part, wide), *range(REACH, REACH + part)]:
            here = first[row, pl.ds(start, EDGE), :]
            if row < REACH:
                here = pltpu.roll(jnp.where(high_lanes, here, first[row + part, pl.ds(start, EDGE), :]), levels, 1)
            elif row >= REACH + part:
                here = pltpu.roll(jnp.where(low_lanes, here, first[row - part, pl.ds(start, EDGE), :]), LANES - levels, 1)
            mask = mask_y
            if not REACH <= row < REACH + part:
                mask = jnp.logical_and(mask, inside_x(row, REACH, part))
            first[row, pl.ds(start, EDGE), :] = jnp.where(mask, here, 0.0)

    south_mask = inside_y(FRONT - EDGE, EDGE, cols)
    north_mask = inside_y(end, EDGE, cols)
    half = cols // 2
    source, dest = first, second
    for step in range(1, SUB + 1):
        def one_row(row, source=source, dest=dest, last=step == SUB):
            mask_x = inside_x(row, REACH, part)
            pieces = [(FRONT, half, None), (FRONT + half, cols - half, None)]
            if not last:
                pieces += [(FRONT - EDGE, EDGE, south_mask), (end, EDGE, north_mask)]
            for start, count, mask_y in pieces:
                value = advance(source, row, start, count, fine_constants)
                mask = mask_x if mask_y is None else jnp.logical_and(mask_x, mask_y)
                if not (last and mask_y is None):
                    value = jnp.where(mask, value, 0.0)
                dest[row, pl.ds(start, count), :] = value

        pl.loop(step, wide - step)(one_row)
        source, dest = dest, source
    fine = source

    for row in range(part_c):
        fine_mean[row] = restricted(fine, row)

    count_c = cols_c + 2 * EDGE
    begin_c = FRONT - EDGE
    mask_y = inside_y(begin_c, count_c, cols_c)

    def extend(buffer):
        for row in range(wide_c):
            here = buffer[row, pl.ds(begin_c, count_c), :]
            if row < COARSE_REACH:
                here = pltpu.roll(
                    jnp.where(high_lanes, here, buffer[row + part_c, pl.ds(begin_c, count_c), :]), levels, 1
                )
            elif row >= COARSE_REACH + part_c:
                here = pltpu.roll(
                    jnp.where(low_lanes, here, buffer[row - part_c, pl.ds(begin_c, count_c), :]), LANES - levels, 1
                )
            mask = jnp.logical_and(mask_y, inside_x(row, COARSE_REACH, part_c))
            extended[row, pl.ds(begin_c, count_c), :] = jnp.where(mask, here, 0.0)

    all_arrived(old_copies, 0, AROUND)
    sends_done(old_copies, 0, AROUND)
    extend(old_wide)
    for row in range(1, wide_c - 1):
        old_image[row - 1] = advance(extended, row, begin_c, count_c, coarse_constants)

    @pl.when(tm > 0)
    def _():
        all_arrived(chain_copies, 1, PLANE)
        extend(new_wide)

    for row in range(1, wide_c - 1):
        moved = advance(extended, row, begin_c, count_c, coarse_constants) - old_image[row - 1]
        mask = jnp.logical_and(mask_y, inside_x(row, COARSE_REACH, part_c))
        change[row - 1, pl.ds(begin_c, count_c), :] = jnp.where(mask, moved, 0.0)

    def change_row(row):
        return change[row, pl.ds(begin_c, count_c), :]

    @pl.when(tm < n_tm - 1)
    def _():
        for row in range(part_c):
            line[pl.ds(begin_c, count_c), :] = (
                mean_side * (change_row(row) + change_row(row + 2)) + mean_mid * change_row(row + 1)
            )
            sides = line[pl.ds(FRONT - 1, cols_c), :] + line[pl.ds(FRONT + 1, cols_c), :]
            sent[row] = fine_mean[row] + mean_side * sides + mean_mid * line[pl.ds(FRONT, cols_c), :]
        send_all(chain_copies, 1, PLANE)

    def blend(offset, low, mid, high):
        total = weights_mid[offset] * mid
        if weights_low[offset]:
            total = total + weights_low[offset] * low
        if weights_high[offset]:
            total = total + weights_high[offset] * high
        return total

    for row in range(part):
        at, offset = row // RATIO, row % RATIO
        line[pl.ds(begin_c, count_c), :] = blend(offset, change_row(at), change_row(at + 1), change_row(at + 2))
        low, mid, high = (line[pl.ds(FRONT + d, cols_c), :] for d in (-1, 0, 1))
        for o in range(RATIO):
            fine_line[pl.ds(o, cols_c, stride=RATIO), :] = blend(o, low, mid, high)
        ending = (fine[REACH + row, pl.ds(FRONT, cols), :] + fine_line[...]).T
        for p in range(packs):
            out_ref[pl.ds(p * part + row, levels, stride=rows), :] = ending[p * levels : (p + 1) * levels]

    pl.when(tm < n_tm - 1)(lambda: sends_done(chain_copies, 1, PLANE))


def shards(sizes, state_starts, diffusivity, wind):
    _, levels, rows, cols = state_starts.shape
    packs = LANES // levels
    part = rows // packs
    part_c = part // RATIO
    cols_c = cols // RATIO
    wide, wide_c = part + 2 * REACH, part_c + 2 * COARSE_REACH
    vmem = functools.partial(pltpu.VMEM, dtype=jnp.float32)
    scratch = [
        vmem((wide, cols + 2 * FRONT, LANES)),
        vmem((wide, cols + 2 * FRONT, LANES)),
        vmem((2, REACH, levels, cols)),
        vmem((2, REACH, levels, cols)),
        vmem((wide_c, cols_c + 2 * FRONT, LANES)),
        vmem((wide_c, cols_c + 2 * FRONT, LANES)),
        vmem((wide_c, cols_c + 2 * FRONT, LANES)),
        vmem((wide_c - 2, cols_c + 2 * EDGE, LANES)),
        vmem((wide_c - 2, cols_c + 2 * FRONT, LANES)),
        vmem((part_c, cols_c, LANES)),
        vmem((part_c, cols_c, LANES)),
        vmem((cols_c + 2 * FRONT, LANES)),
        vmem((cols, LANES)),
    ] + [pltpu.SemaphoreType.DMA((9,))] * 6
    in_vmem = pl.BlockSpec(memory_space=pltpu.VMEM)
    ending = pl.pallas_call(
        functools.partial(kernel, sizes, levels, rows, cols),
        out_shape=pltpu.VMEM((levels * rows, cols), jnp.float32),
        in_specs=[in_vmem] * 3,
        out_specs=in_vmem,
        scratch_shapes=scratch,
        compiler_params=pltpu.CompilerParams(collective_id=0, has_side_effects=True),
        name="parareal",
    )(state_starts.reshape(levels * rows, cols), diffusivity.reshape(1, levels), wind)
    return ending.reshape(1, levels, rows, cols)


def solution(mesh):
    sizes = tuple(mesh.shape[axis] for axis in ("tm", "gx", "gy"))
    placed = (P("tm", None, "gx", "gy"), P(), P())
    return jax.shard_map(
        functools.partial(shards, sizes),
        mesh=mesh, in_specs=placed, out_specs=P("tm", None, "gx", "gy"), check_vma=False,
    )
```

```python
import functools

import jax
import jax.numpy as jnp
from jax import lax
from jax.experimental import pallas as pl
from jax.experimental.pallas import tpu as pltpu
from jax.sharding import PartitionSpec as P

SUB = 4
REACH = SUB
RATIO = 4
LANES = 128
EDGE = 8
FRONT = 2 * EDGE
COARSE_REACH = 2

time_step = 0.2
weights_low = (0.375, 0.125, 0.0, 0.0)
weights_mid = (0.625, 0.875, 0.875, 0.625)
weights_high = (0.0, 0.0, 0.125, 0.375)
mean_side, mean_mid = 0.125, 0.75

PLANE = tuple((dx, dy) for dx in (-1, 0, 1) for dy in (-1, 0, 1))
AROUND = tuple(d for d in PLANE if d != (0, 0))


def conjunction(conditions):
    total = True
    for condition in conditions:
        total = condition if total is True else jnp.logical_and(total, condition)
    return total


def kernel(
    sizes, levels, rows, cols,
    x_hbm, diff_ref, wind_ref, out_ref,
    x_ref, load_sem,
    first, second, x_send, x_recv, old_wide, new_wide, extended, old_image, change,
    sent, fine_mean, line, fine_line, raw_edge, spread_rows,
    fine_out, fine_in, old_out, old_in, chain_out, chain_in,
):
    n_tm, n_gx, n_gy = sizes
    tm, gx, gy = lax.axis_index("tm"), lax.axis_index("gx"), lax.axis_index("gy")
    packs = LANES // levels
    part = rows // packs
    part_c = part // RATIO
    cols_c = cols // RATIO
    wide = part + 2 * REACH
    wide_c = part_c + 2 * COARSE_REACH
    end = FRONT + cols
    end_c = FRONT + cols_c

    def there(dz, dx, dy):
        tests = []
        for place, move, count in ((tm, dz, n_tm), (gx, dx, n_gx), (gy, dy, n_gy)):
            if move < 0:
                tests.append(place > 0)
            if move > 0:
                tests.append(place < count - 1)
        return conjunction(tests)

    def guarded(condition, action):
        if condition is True:
            action()
        else:
            pl.when(condition)(action)

    def target(dz, dx, dy):
        return (tm + dz, gx + dx, gy + dy)

    load = pltpu.make_async_copy(x_hbm, x_ref, load_sem)
    load.start()

    barrier = pltpu.get_barrier_semaphore()
    partners = [(dz, dx, dy) for dz in (-1, 0, 1) for dx, dy in PLANE if (dz, dx, dy) != (0, 0, 0)]
    awaited = jnp.int32(0)
    for move in partners:
        def greet(move=move):
            pl.semaphore_signal(barrier, inc=1, device_id=target(*move), device_id_type=pl.DeviceIdType.MESH)
        guarded(there(*move), greet)
        awaited = awaited + there(*move).astype(jnp.int32)

    def send_all(copies, dz, moves):
        for move in moves:
            guarded(there(dz, *move), lambda move=move: copies[move].start())

    def sends_done(copies, dz, moves):
        for move in moves:
            guarded(there(dz, *move), lambda move=move: copies[move].wait_send())

    def all_arrived(copies, dz, moves):
        for dx, dy in moves:
            guarded(there(-dz, -dx, -dy), lambda move=(dx, dy): copies[move].wait_recv())

    def remote(source, landing, out_sem, in_sem, move):
        return pltpu.make_async_remote_copy(
            src_ref=source, dst_ref=landing, send_sem=out_sem, recv_sem=in_sem,
            device_id=target(*move), device_id_type=pl.DeviceIdType.MESH,
        )

    def index_of(move):
        return (move[0] + 1) * 3 + move[1] + 1

    fine_copies = {}
    for move in AROUND:
        dx, dy = move
        k = index_of(move)
        if dy == 0:
            source, landing = x_send.at[(dx + 1) // 2], x_recv.at[(dx + 1) // 2]
        else:
            take_row, put_row, height = {
                0: (REACH, REACH, part), -1: (REACH, REACH + part, REACH), 1: (part, 0, REACH)
            }[dx]
            take, put = {-1: (FRONT, end), 1: (end - EDGE, FRONT - EDGE)}[dy]
            source = first.at[pl.ds(take_row, height), pl.ds(take, EDGE)]
            landing = first.at[pl.ds(put_row, height), pl.ds(put, EDGE)]
        fine_copies[move] = remote(source, landing, fine_out.at[k], fine_in.at[k], (0, dx, dy))

    def coarse_copies(buffer, row0, col0, landing_buffer, out_sems, in_sems, dz, moves):
        copies = {}
        for move in moves:
            dx, dy = move
            k = index_of(move)
            take_row, put_row, height = {
                0: (0, COARSE_REACH, part_c),
                -1: (0, COARSE_REACH + part_c, COARSE_REACH),
                1: (part_c - COARSE_REACH, 0, COARSE_REACH),
            }[dx]
            take, put, width = {
                0: (0, FRONT, cols_c), -1: (0, end_c, EDGE), 1: (cols_c - EDGE, FRONT - EDGE, EDGE)
            }[dy]
            copies[move] = remote(
                buffer.at[pl.ds(row0 + take_row, height), pl.ds(col0 + take, width)],
                landing_buffer.at[pl.ds(put_row, height), pl.ds(put, width)],
                out_sems.at[k], in_sems.at[k], (dz, dx, dy),
            )
        return copies

    old_copies = coarse_copies(old_wide, COARSE_REACH, FRONT, old_wide, old_out, old_in, 0, AROUND)
    chain_copies = coarse_copies(sent, 0, 0, new_wide, chain_out, chain_in, 1, PLANE)

    lane = lax.broadcasted_iota(jnp.int32, (1, LANES), 1)
    pack = lane // levels

    def packed(row):
        return jnp.concatenate([row] * packs, axis=1)

    diffuse = packed(diff_ref[...])
    east_wind = packed(wind_ref[0:1, :])
    north_wind = packed(wind_ref[1:2, :])

    def constants(factor):
        spread = (time_step * factor) * diffuse
        return 1.0 - 4.0 * spread, spread, (0.5 * time_step) * east_wind, (0.5 * time_step) * north_wind

    fine_constants = constants(1.0)
    coarse_constants = constants(0.25)

    def advance(source, row, start, count, consts):
        keep, spread, along_x, along_y = consts
        centre = source[row, pl.ds(start, count), :]
        east = source[row + 1, pl.ds(start, count), :]
        west = source[row - 1, pl.ds(start, count), :]
        north = source[row, pl.ds(start + 1, count), :]
        south = source[row, pl.ds(start - 1, count), :]
        pushed = along_x * (east - west) + along_y * (north - south)
        return centre * (keep - pushed) + spread * ((east + west) + (north + south))

    def native_row(x):
        if x < 0:
            return x_recv[1, x + REACH]
        if x >= rows:
            return x_recv[0, x - rows]
        return x_ref[pl.ds(x, levels, stride=rows), :]

    def bring_in(row):
        stacked = jnp.concatenate([native_row(p * part + row - REACH) for p in range(packs)], axis=0)
        first[row, pl.ds(FRONT, cols), :] = stacked.T

    load.wait()
    for r in range(REACH):
        x_send[0, r] = native_row(r)
        x_send[1, r] = native_row(rows - REACH + r)
    pl.semaphore_wait(barrier, awaited)
    x_moves = tuple(m for m in AROUND if m[1] == 0)
    y_moves = tuple(m for m in AROUND if m[1] != 0)
    send_all(fine_copies, 0, x_moves)
    for row in range(REACH, REACH + part):
        bring_in(row)
    send_all(fine_copies, 0, y_moves)

    def restricted(source, row):
        total = source[REACH + row * RATIO, pl.ds(FRONT, cols), :]
        for r in range(1, RATIO):
            total = total + source[REACH + row * RATIO + r, pl.ds(FRONT, cols), :]
        fine_line[...] = total
        mean = fine_line[pl.ds(0, cols_c, stride=RATIO), :]
        for o in range(1, RATIO):
            mean = mean + fine_line[pl.ds(o, cols_c, stride=RATIO), :]
        return mean * (1.0 / RATIO**2)

    for row in range(part_c):
        old_wide[COARSE_REACH + row, pl.ds(FRONT, cols_c), :] = restricted(first, row)
    send_all(old_copies, 0, AROUND)

    def inside_x(row, reach, length):
        place = (gx * packs + pack) * length + (row - reach)
        return jnp.logical_and(place >= 0, place < n_gx * packs * length)

    def inside_y(start, count, length):
        place = gy * length + (start - FRONT) + lax.broadcasted_iota(jnp.int32, (count, LANES), 0)
        return jnp.logical_and(place >= 0, place < n_gy * length)

    low_lanes = lane < levels
    high_lanes = lane >= LANES - levels
    side_moves = tuple(m for m in AROUND if m[0] == 0)
    corner_moves = tuple(m for m in y_moves if m[0] != 0)
    edges = ((FRONT - EDGE, inside_y(FRONT - EDGE, EDGE, cols)), (end, inside_y(end, EDGE, cols)))
    halo_rows = [*range(REACH), *range(REACH + part, wide)]
    half = cols // 2

    def update(source, dest, row, consts, last):
        for start, count in ((FRONT, half), (FRONT + half, cols - half)):
            dest[row, pl.ds(start, count), :] = advance(source, row, start, count, consts)
        if not last:
            for start, mask in edges:
                value = advance(source, row, start, EDGE, consts)
                dest[row, pl.ds(start, EDGE), :] = jnp.where(mask, value, 0.0)

    buffers = (first, second)

    all_arrived(fine_copies, 0, side_moves)
    def edge_of(start):
        return 0 if start < FRONT else 1

    for start, mask in edges:
        for row in [*range(REACH), *range(part - REACH, part)]:
            raw_edge[edge_of(start), row] = first[row + REACH, pl.ds(start, EDGE), :]
        for row in range(REACH, REACH + part):
            first[row, pl.ds(start, EDGE), :] = jnp.where(mask, first[row, pl.ds(start, EDGE), :], 0.0)
    for step in range(1, SUB + 1):
        def inner_row(row, step=step):
            update(buffers[(step - 1) % 2], buffers[step % 2], row, fine_constants, step == SUB)

        sends_done(fine_copies, 0, y_moves) if step == 2 else None
        pl.loop(REACH + step, REACH + part - step)(inner_row)

    all_arrived(fine_copies, 0, x_moves)
    for row in halo_rows:
        bring_in(row)
        inner = first[row, pl.ds(FRONT, cols), :]
        first[row, pl.ds(FRONT, cols), :] = jnp.where(inside_x(row, REACH, part), inner, 0.0)
    all_arrived(fine_copies, 0, corner_moves)
    for start, mask_y in edges:
        for row in halo_rows:
            here = first[row, pl.ds(start, EDGE), :]
            if row < REACH:
                here = pltpu.roll(jnp.where(high_lanes, here, raw_edge[edge_of(start), row + part - REACH]), levels, 1)
            else:
                here = pltpu.roll(jnp.where(low_lanes, here, raw_edge[edge_of(start), row - part - REACH]), LANES - levels, 1)
            mask = jnp.logical_and(mask_y, inside_x(row, REACH, part))
            first[row, pl.ds(start, EDGE), :] = jnp.where(mask, here, 0.0)
    for step in range(1, SUB + 1):
        def outer_row(row, step=step):
            for shifted in (row, row + part + REACH - 2 * step):
                mask_x = inside_x(shifted, REACH, part)
                consts = tuple(jnp.where(mask_x, c, 0.0) for c in fine_constants)
                update(buffers[(step - 1) % 2], buffers[step % 2], shifted, consts, step == SUB)

        pl.loop(step, REACH + step)(outer_row)
    sends_done(fine_copies, 0, x_moves)
    fine = buffers[SUB % 2]

    for row in range(part_c):
        fine_mean[row] = restricted(fine, row)

    count_c = cols_c + 2 * EDGE
    begin_c = FRONT - EDGE
    mask_y = inside_y(begin_c, count_c, cols_c)

    def extend(buffer):
        for row in range(wide_c):
            here = buffer[row, pl.ds(begin_c, count_c), :]
            if row < COARSE_REACH:
                here = pltpu.roll(
                    jnp.where(high_lanes, here, buffer[row + part_c, pl.ds(begin_c, count_c), :]), levels, 1
                )
            elif row >= COARSE_REACH + part_c:
                here = pltpu.roll(
                    jnp.where(low_lanes, here, buffer[row - part_c, pl.ds(begin_c, count_c), :]), LANES - levels, 1
                )
            mask = jnp.logical_and(mask_y, inside_x(row, COARSE_REACH, part_c))
            extended[row, pl.ds(begin_c, count_c), :] = jnp.where(mask, here, 0.0)

    all_arrived(old_copies, 0, AROUND)
    sends_done(old_copies, 0, AROUND)
    extend(old_wide)
    for row in range(1, wide_c - 1):
        old_image[row - 1] = advance(extended, row, begin_c, count_c, coarse_constants)

    def write_fine():
        for row in range(part):
            turned = fine[REACH + row, pl.ds(FRONT, cols), :].T
            for p in range(packs):
                out_ref[pl.ds(p * part + row, levels, stride=rows), :] = turned[p * levels : (p + 1) * levels]

    @pl.when(tm > 0)
    def _():
        write_fine()
        all_arrived(chain_copies, 1, PLANE)
        extend(new_wide)

    for row in range(1, wide_c - 1):
        moved = advance(extended, row, begin_c, count_c, coarse_constants) - old_image[row - 1]
        mask = jnp.logical_and(mask_y, inside_x(row, COARSE_REACH, part_c))
        change[row - 1, pl.ds(begin_c, count_c), :] = jnp.where(mask, moved, 0.0)

    def change_row(row):
        return change[row, pl.ds(begin_c, count_c), :]

    @pl.when(tm < n_tm - 1)
    def _():
        for row in range(part_c):
            line[pl.ds(begin_c, count_c), :] = (
                mean_side * (change_row(row) + change_row(row + 2)) + mean_mid * change_row(row + 1)
            )
            sides = line[pl.ds(FRONT - 1, cols_c), :] + line[pl.ds(FRONT + 1, cols_c), :]
            sent[row] = fine_mean[row] + mean_side * sides + mean_mid * line[pl.ds(FRONT, cols_c), :]
        send_all(chain_copies, 1, PLANE)

    pl.when(tm == 0)(write_fine)

    coarse_col = lax.broadcasted_iota(jnp.int32, (count_c, cols), 0) - EDGE
    fine_col = lax.broadcasted_iota(jnp.int32, (count_c, cols), 1)
    offset_of = fine_col & (RATIO - 1)
    apart = coarse_col - (fine_col >> (RATIO.bit_length() - 1))
    spreading = jnp.zeros((count_c, cols), jnp.float32)
    for o in range(RATIO):
        for distance, weights in ((-1, weights_low), (0, weights_mid), (1, weights_high)):
            chosen = jnp.logical_and(offset_of == o, apart == distance)
            spreading = jnp.where(chosen, weights[o], spreading)
    for row in range(part_c + 2):
        spread_rows[row] = jnp.dot(
            change_row(row).T, spreading, precision=lax.Precision.HIGHEST, preferred_element_type=jnp.float32
        )

    for row in range(part):
        at, o = row // RATIO, row % RATIO
        total = weights_mid[o] * spread_rows[at + 1]
        if weights_low[o]:
            total = total + weights_low[o] * spread_rows[at]
        if weights_high[o]:
            total = total + weights_high[o] * spread_rows[at + 2]
        for p in range(packs):
            place = pl.ds(p * part + row, levels, stride=rows)
            out_ref[place, :] = out_ref[place, :] + total[p * levels : (p + 1) * levels]

    pl.when(tm < n_tm - 1)(lambda: sends_done(chain_copies, 1, PLANE))


def shards(sizes, state_starts, diffusivity, wind):
    _, levels, rows, cols = state_starts.shape
    packs = LANES // levels
    part = rows // packs
    part_c = part // RATIO
    cols_c = cols // RATIO
    wide, wide_c = part + 2 * REACH, part_c + 2 * COARSE_REACH
    vmem = functools.partial(pltpu.VMEM, dtype=jnp.float32)
    scratch = [
        vmem((levels * rows, cols)),
        pltpu.SemaphoreType.DMA,
        vmem((wide, cols + 2 * FRONT, LANES)),
        vmem((wide, cols + 2 * FRONT, LANES)),
        vmem((2, REACH, levels, cols)),
        vmem((2, REACH, levels, cols)),
        vmem((wide_c, cols_c + 2 * FRONT, LANES)),
        vmem((wide_c, cols_c + 2 * FRONT, LANES)),
        vmem((wide_c, cols_c + 2 * FRONT, LANES)),
        vmem((wide_c - 2, cols_c + 2 * EDGE, LANES)),
        vmem((wide_c - 2, cols_c + 2 * FRONT, LANES)),
        vmem((part_c, cols_c, LANES)),
        vmem((part_c, cols_c, LANES)),
        vmem((cols_c + 2 * FRONT, LANES)),
        vmem((cols, LANES)),
        vmem((2, part, EDGE, LANES)),
        vmem((part_c + 2, LANES, cols)),
    ] + [pltpu.SemaphoreType.DMA((9,))] * 6
    in_vmem = pl.BlockSpec(memory_space=pltpu.VMEM)
    ending = pl.pallas_call(
        functools.partial(kernel, sizes, levels, rows, cols),
        out_shape=pltpu.VMEM((levels * rows, cols), jnp.float32),
        in_specs=[pl.BlockSpec(memory_space=pl.ANY), in_vmem, in_vmem],
        out_specs=in_vmem,
        scratch_shapes=scratch,
        compiler_params=pltpu.CompilerParams(collective_id=0, has_side_effects=True),
        name="parareal",
    )(state_starts.reshape(levels * rows, cols), diffusivity.reshape(1, levels), wind)
    return ending.reshape(1, levels, rows, cols)


def solution(mesh):
    sizes = tuple(mesh.shape[axis] for axis in ("tm", "gx", "gy"))
    placed = (P("tm", None, "gx", "gy"), P(), P())
    return jax.shard_map(
        functools.partial(shards, sizes),
        mesh=mesh, in_specs=placed, out_specs=P("tm", None, "gx", "gy"), check_vma=False,
    )
```

```python
import functools

import jax
import jax.numpy as jnp
from jax import lax
from jax.experimental import pallas as pl
from jax.experimental.pallas import tpu as pltpu
from jax.sharding import PartitionSpec as P

SUB = 4
REACH = SUB
RATIO = 4
LANES = 128
EDGE = 8
FRONT = 2 * EDGE
COARSE_REACH = 2

time_step = 0.2
weights_low = (0.375, 0.125, 0.0, 0.0)
weights_mid = (0.625, 0.875, 0.875, 0.625)
weights_high = (0.0, 0.0, 0.125, 0.375)
mean_side, mean_mid = 0.125, 0.75

PLANE = tuple((dx, dy) for dx in (-1, 0, 1) for dy in (-1, 0, 1))
AROUND = tuple(d for d in PLANE if d != (0, 0))


def conjunction(conditions):
    total = True
    for condition in conditions:
        total = condition if total is True else jnp.logical_and(total, condition)
    return total


def kernel(
    sizes, levels, rows, cols,
    x_hbm, diff_ref, wind_ref, out_ref,
    x_ref, load_sem,
    first, second, x_send, x_recv, old_wide, new_wide, extended, old_image, change,
    sent, fine_mean, line, fine_line, raw_edge, spread_rows,
    fine_out, fine_in, old_out, old_in, chain_out, chain_in, *strip_refs,
):
    n_tm, n_gx, n_gy = sizes
    tm, gx, gy = lax.axis_index("tm"), lax.axis_index("gx"), lax.axis_index("gy")
    packs = LANES // levels
    part = rows // packs
    part_c = part // RATIO
    cols_c = cols // RATIO
    wide = part + 2 * REACH
    wide_c = part_c + 2 * COARSE_REACH
    end = FRONT + cols
    end_c = FRONT + cols_c

    def there(dz, dx, dy):
        tests = []
        for place, move, count in ((tm, dz, n_tm), (gx, dx, n_gx), (gy, dy, n_gy)):
            if move < 0:
                tests.append(place > 0)
            if move > 0:
                tests.append(place < count - 1)
        return conjunction(tests)

    def guarded(condition, action):
        if condition is True:
            action()
        else:
            pl.when(condition)(action)

    def target(dz, dx, dy):
        return (tm + dz, gx + dx, gy + dy)

    load = pltpu.make_async_copy(x_hbm, x_ref, load_sem)
    load.start()

    barrier = pltpu.get_barrier_semaphore()
    partners = [(dz, dx, dy) for dz in (-1, 0, 1) for dx, dy in PLANE if (dz, dx, dy) != (0, 0, 0)]
    partners.sort(key=lambda move: -sum(map(abs, move)))
    awaited = jnp.int32(0)
    for move in partners:
        def greet(move=move):
            pl.semaphore_signal(barrier, inc=1, device_id=target(*move), device_id_type=pl.DeviceIdType.MESH)
        guarded(there(*move), greet)
        awaited = awaited + there(*move).astype(jnp.int32)

    def send_all(copies, dz, moves):
        for move in moves:
            guarded(there(dz, *move), lambda move=move: copies[move].start())

    def sends_done(copies, dz, moves):
        for move in moves:
            guarded(there(dz, *move), lambda move=move: copies[move].wait_send())

    def all_arrived(copies, dz, moves):
        for dx, dy in moves:
            guarded(there(-dz, -dx, -dy), lambda move=(dx, dy): copies[move].wait_recv())

    def remote(source, landing, out_sem, in_sem, move):
        return pltpu.make_async_remote_copy(
            src_ref=source, dst_ref=landing, send_sem=out_sem, recv_sem=in_sem,
            device_id=target(*move), device_id_type=pl.DeviceIdType.MESH,
        )

    def index_of(move):
        return (move[0] + 1) * 3 + move[1] + 1

    fine_copies = {}
    for move in AROUND:
        dx, dy = move
        k = index_of(move)
        if dy == 0:
            source, landing = x_send.at[(dx + 1) // 2], x_recv.at[(dx + 1) // 2]
        else:
            take_row, put_row, height = {
                0: (REACH, REACH, part), -1: (REACH, REACH + part, REACH), 1: (part, 0, REACH)
            }[dx]
            take, put = {-1: (FRONT, end), 1: (end - EDGE, FRONT - EDGE)}[dy]
            source = first.at[pl.ds(take_row, height), pl.ds(take, EDGE)]
            landing = first.at[pl.ds(put_row, height), pl.ds(put, EDGE)]
        fine_copies[move] = remote(source, landing, fine_out.at[k], fine_in.at[k], (0, dx, dy))

    def coarse_copies(main, wide_in, strips, out_sems, in_sems, dz):
        row_out, row_in, side_out, side_in, corner_out, corner_in = strips
        copies = {}
        for dx, dy in PLANE if dz else AROUND:
            k = index_of((dx, dy))
            towards_x, towards_y = (dx + 1) // 2, (dy + 1) // 2
            if dx == 0 and dy == 0:
                source, landing = main, wide_in.at[pl.ds(COARSE_REACH, part_c), pl.ds(FRONT, cols_c)]
            elif dy == 0:
                source, landing = row_out.at[towards_x], row_in.at[towards_x, pl.ds(FRONT, cols_c)]
            elif dx == 0:
                source, landing = side_out.at[towards_y], side_in.at[towards_y]
            else:
                source, landing = corner_out.at[towards_x, towards_y], corner_in.at[towards_x, towards_y]
            copies[dx, dy] = remote(source, landing, out_sems.at[k], in_sems.at[k], (dz, dx, dy))
        return copies

    old_strips, new_strips = strip_refs[:6], strip_refs[6:]
    old_copies = coarse_copies(None, old_wide, old_strips, old_out, old_in, 0)
    chain_copies = coarse_copies(sent, new_wide, new_strips, chain_out, chain_in, 1)

    lane = lax.broadcasted_iota(jnp.int32, (1, LANES), 1)
    pack = lane // levels

    def packed(row):
        return jnp.concatenate([row] * packs, axis=1)

    diffuse = packed(diff_ref[...])
    east_wind = packed(wind_ref[0:1, :])
    north_wind = packed(wind_ref[1:2, :])

    def constants(factor):
        spread = (time_step * factor) * diffuse
        return 1.0 - 4.0 * spread, spread, (0.5 * time_step) * east_wind, (0.5 * time_step) * north_wind

    fine_constants = constants(1.0)
    coarse_constants = constants(0.25)

    def advance(source, row, start, count, consts):
        keep, spread, along_x, along_y = consts
        centre = source[row, pl.ds(start, count), :]
        east = source[row + 1, pl.ds(start, count), :]
        west = source[row - 1, pl.ds(start, count), :]
        north = source[row, pl.ds(start + 1, count), :]
        south = source[row, pl.ds(start - 1, count), :]
        pushed = along_x * (east - west) + along_y * (north - south)
        return centre * (keep - pushed) + spread * ((east + west) + (north + south))

    def native_row(x):
        if x < 0:
            return x_recv[1, x + REACH]
        if x >= rows:
            return x_recv[0, x - rows]
        return x_ref[pl.ds(x, levels, stride=rows), :]

    def bring_in(row):
        stacked = jnp.concatenate([native_row(p * part + row - REACH) for p in range(packs)], axis=0)
        first[row, pl.ds(FRONT, cols), :] = stacked.T

    load.wait()
    for r in range(REACH):
        x_send[0, r] = native_row(r)
        x_send[1, r] = native_row(rows - REACH + r)
    x_moves = tuple(m for m in AROUND if m[1] == 0)
    y_moves = tuple(m for m in AROUND if m[1] != 0)
    low_lanes = lane < levels
    high_lanes = lane >= LANES - levels
    for row in range(REACH, REACH + part):
        bring_in(row)

    def restricted(source, row):
        total = source[REACH + row * RATIO, pl.ds(FRONT, cols), :]
        for r in range(1, RATIO):
            total = total + source[REACH + row * RATIO + r, pl.ds(FRONT, cols), :]
        fine_line[...] = total
        mean = fine_line[pl.ds(0, cols_c, stride=RATIO), :]
        for o in range(1, RATIO):
            mean = mean + fine_line[pl.ds(o, cols_c, stride=RATIO), :]
        return mean * (1.0 / RATIO**2)

    def swapped(value):
        return pltpu.roll(value, levels, 1)

    def pack_strips(row_of, strips):
        row_out, _, side_out, _, corner_out, _ = strips
        row_out[0] = jnp.where(low_lanes, row_of(0, 0, cols_c), swapped(row_of(1, 0, cols_c)))
        row_out[1] = jnp.where(low_lanes, swapped(row_of(part_c - 2, 0, cols_c)), row_of(part_c - 1, 0, cols_c))
        for side, col in ((0, 0), (1, cols_c - COARSE_REACH)):
            for row in range(part_c):
                side_out[side, pl.ds(COARSE_REACH * row, COARSE_REACH), :] = row_of(row, col, COARSE_REACH)
            for towards in range(2):
                corner_out[towards, side, pl.ds(0, COARSE_REACH), :] = row_out[towards, pl.ds(col, COARSE_REACH), :]

    def old_row(row, col, count):
        return old_wide[COARSE_REACH + row, pl.ds(FRONT + col, count), :]

    for row in range(part_c):
        old_wide[COARSE_REACH + row, pl.ds(FRONT, cols_c), :] = restricted(first, row)
    pack_strips(old_row, old_strips)
    pl.semaphore_wait(barrier, awaited)
    send_all(fine_copies, 0, y_moves)
    send_all(fine_copies, 0, x_moves)
    send_all(old_copies, 0, AROUND)

    def inside_x(row, reach, length):
        place = (gx * packs + pack) * length + (row - reach)
        return jnp.logical_and(place >= 0, place < n_gx * packs * length)

    def inside_y(start, count, length):
        place = gy * length + (start - FRONT) + lax.broadcasted_iota(jnp.int32, (count, LANES), 0)
        return jnp.logical_and(place >= 0, place < n_gy * length)

    side_moves = tuple(m for m in AROUND if m[0] == 0)
    corner_moves = tuple(m for m in y_moves if m[0] != 0)
    edges = ((FRONT - EDGE, inside_y(FRONT - EDGE, EDGE, cols)), (end, inside_y(end, EDGE, cols)))
    halo_rows = [*range(REACH), *range(REACH + part, wide)]
    half = cols // 2

    def update(source, dest, row, consts, last):
        for start, count in ((FRONT, half), (FRONT + half, cols - half)):
            dest[row, pl.ds(start, count), :] = advance(source, row, start, count, consts)
        if not last:
            for start, mask in edges:
                value = advance(source, row, start, EDGE, consts)
                dest[row, pl.ds(start, EDGE), :] = jnp.where(mask, value, 0.0)

    buffers = (first, second)

    all_arrived(fine_copies, 0, side_moves)
    def edge_of(start):
        return 0 if start < FRONT else 1

    for start, mask in edges:
        for row in [*range(REACH), *range(part - REACH, part)]:
            raw_edge[edge_of(start), row] = first[row + REACH, pl.ds(start, EDGE), :]
        for row in range(REACH, REACH + part):
            first[row, pl.ds(start, EDGE), :] = jnp.where(mask, first[row, pl.ds(start, EDGE), :], 0.0)
    for step in range(1, SUB + 1):
        def inner_row(row, step=step):
            update(buffers[(step - 1) % 2], buffers[step % 2], row, fine_constants, step == SUB)

        sends_done(fine_copies, 0, y_moves) if step == 2 else None
        pl.loop(REACH + step, REACH + part - step)(inner_row)

    all_arrived(fine_copies, 0, x_moves)
    for row in halo_rows:
        bring_in(row)
        inner = first[row, pl.ds(FRONT, cols), :]
        first[row, pl.ds(FRONT, cols), :] = jnp.where(inside_x(row, REACH, part), inner, 0.0)
    all_arrived(fine_copies, 0, corner_moves)
    for start, mask_y in edges:
        for row in halo_rows:
            here = first[row, pl.ds(start, EDGE), :]
            if row < REACH:
                here = pltpu.roll(jnp.where(high_lanes, here, raw_edge[edge_of(start), row + part - REACH]), levels, 1)
            else:
                here = pltpu.roll(jnp.where(low_lanes, here, raw_edge[edge_of(start), row - part - REACH]), LANES - levels, 1)
            mask = jnp.logical_and(mask_y, inside_x(row, REACH, part))
            first[row, pl.ds(start, EDGE), :] = jnp.where(mask, here, 0.0)
    for step in range(1, SUB + 1):
        def outer_row(row, step=step):
            for shifted in (row, row + part + REACH - 2 * step):
                mask_x = inside_x(shifted, REACH, part)
                consts = tuple(jnp.where(mask_x, c, 0.0) for c in fine_constants)
                update(buffers[(step - 1) % 2], buffers[step % 2], shifted, consts, step == SUB)

        pl.loop(step, REACH + step)(outer_row)
    sends_done(fine_copies, 0, x_moves)
    fine = buffers[SUB % 2]

    for row in range(part_c):
        fine_mean[row] = restricted(fine, row)

    count_c = cols_c + 2 * EDGE
    begin_c = FRONT - EDGE
    mask_y = inside_y(begin_c, count_c, cols_c)

    def extend(buffer, strips):
        _, row_in, _, side_in, _, corner_in = strips
        for side, col in ((0, end_c), (1, FRONT - COARSE_REACH)):
            for row in range(part_c):
                buffer[COARSE_REACH + row, pl.ds(col, COARSE_REACH), :] = side_in[
                    side, pl.ds(COARSE_REACH * row, COARSE_REACH), :
                ]
            for towards in range(2):
                row_in[towards, pl.ds(col, COARSE_REACH), :] = corner_in[towards, side, pl.ds(0, COARSE_REACH), :]

        def own(row):
            return buffer[COARSE_REACH + row, pl.ds(begin_c, count_c), :]

        above, below = (row_in[towards, pl.ds(begin_c, count_c), :] for towards in (0, 1))
        values = [
            jnp.where(low_lanes, below, swapped(own(part_c - 2))),
            swapped(jnp.where(high_lanes, below, own(part_c - 1))),
            *[own(row) for row in range(part_c)],
            swapped(jnp.where(low_lanes, above, own(0))),
            jnp.where(high_lanes, above, swapped(own(1))),
        ]
        for row, value in enumerate(values):
            mask = mask_y
            if not COARSE_REACH <= row < COARSE_REACH + part_c:
                mask = jnp.logical_and(mask_y, inside_x(row, COARSE_REACH, part_c))
            extended[row, pl.ds(begin_c, count_c), :] = jnp.where(mask, value, 0.0)

    all_arrived(old_copies, 0, AROUND)
    sends_done(old_copies, 0, AROUND)
    extend(old_wide, old_strips)
    for row in range(1, wide_c - 1):
        old_image[row - 1] = advance(extended, row, begin_c, count_c, coarse_constants)

    def write_fine():
        for row in range(part):
            turned = fine[REACH + row, pl.ds(FRONT, cols), :].T
            for p in range(packs):
                out_ref[pl.ds(p * part + row, levels, stride=rows), :] = turned[p * levels : (p + 1) * levels]

    @pl.when(tm > 0)
    def _():
        write_fine()
        all_arrived(chain_copies, 1, PLANE)
        extend(new_wide, new_strips)

    for row in range(1, wide_c - 1):
        moved = advance(extended, row, begin_c, count_c, coarse_constants) - old_image[row - 1]
        mask = jnp.logical_and(mask_y, inside_x(row, COARSE_REACH, part_c))
        change[row - 1, pl.ds(begin_c, count_c), :] = jnp.where(mask, moved, 0.0)

    def change_row(row):
        return change[row, pl.ds(begin_c, count_c), :]

    @pl.when(tm < n_tm - 1)
    def _():
        for row in range(part_c):
            line[pl.ds(begin_c, count_c), :] = (
                mean_side * (change_row(row) + change_row(row + 2)) + mean_mid * change_row(row + 1)
            )
            sides = line[pl.ds(FRONT - 1, cols_c), :] + line[pl.ds(FRONT + 1, cols_c), :]
            sent[row] = fine_mean[row] + mean_side * sides + mean_mid * line[pl.ds(FRONT, cols_c), :]
        pack_strips(lambda row, col, count: sent[row, pl.ds(col, count), :], new_strips)
        send_all(chain_copies, 1, AROUND)
        send_all(chain_copies, 1, ((0, 0),))

    pl.when(tm == 0)(write_fine)

    coarse_col = lax.broadcasted_iota(jnp.int32, (count_c, cols), 0) - EDGE
    fine_col = lax.broadcasted_iota(jnp.int32, (count_c, cols), 1)
    offset_of = fine_col & (RATIO - 1)
    apart = coarse_col - (fine_col >> (RATIO.bit_length() - 1))
    spreading = jnp.zeros((count_c, cols), jnp.float32)
    for o in range(RATIO):
        for distance, weights in ((-1, weights_low), (0, weights_mid), (1, weights_high)):
            chosen = jnp.logical_and(offset_of == o, apart == distance)
            spreading = jnp.where(chosen, weights[o], spreading)
    for row in range(part_c + 2):
        spread_rows[row] = jnp.dot(
            change_row(row).T, spreading, precision=lax.Precision.HIGHEST, preferred_element_type=jnp.float32
        )

    for row in range(part):
        at, o = row // RATIO, row % RATIO
        total = weights_mid[o] * spread_rows[at + 1]
        if weights_low[o]:
            total = total + weights_low[o] * spread_rows[at]
        if weights_high[o]:
            total = total + weights_high[o] * spread_rows[at + 2]
        for p in range(packs):
            place = pl.ds(p * part + row, levels, stride=rows)
            out_ref[place, :] = out_ref[place, :] + total[p * levels : (p + 1) * levels]

    pl.when(tm < n_tm - 1)(lambda: sends_done(chain_copies, 1, PLANE))


def shards(sizes, state_starts, diffusivity, wind):
    _, levels, rows, cols = state_starts.shape
    packs = LANES // levels
    if packs != 2 or levels * packs != LANES:
        raise ValueError(levels)
    part = rows // packs
    part_c = part // RATIO
    cols_c = cols // RATIO
    wide, wide_c = part + 2 * REACH, part_c + 2 * COARSE_REACH
    vmem = functools.partial(pltpu.VMEM, dtype=jnp.float32)
    scratch = [
        vmem((levels * rows, cols)),
        pltpu.SemaphoreType.DMA,
        vmem((wide, cols + 2 * FRONT, LANES)),
        vmem((wide, cols + 2 * FRONT, LANES)),
        vmem((2, REACH, levels, cols)),
        vmem((2, REACH, levels, cols)),
        vmem((wide_c, cols_c + 2 * FRONT, LANES)),
        vmem((wide_c, cols_c + 2 * FRONT, LANES)),
        vmem((wide_c, cols_c + 2 * FRONT, LANES)),
        vmem((wide_c - 2, cols_c + 2 * EDGE, LANES)),
        vmem((wide_c - 2, cols_c + 2 * FRONT, LANES)),
        vmem((part_c, cols_c, LANES)),
        vmem((part_c, cols_c, LANES)),
        vmem((cols_c + 2 * FRONT, LANES)),
        vmem((cols, LANES)),
        vmem((2, part, EDGE, LANES)),
        vmem((part_c + 2, LANES, cols)),
    ] + [pltpu.SemaphoreType.DMA((9,))] * 6
    scratch += [
        vmem((2, cols_c, LANES)),
        vmem((2, cols_c + 2 * FRONT, LANES)),
        vmem((2, COARSE_REACH * part_c, LANES)),
        vmem((2, COARSE_REACH * part_c, LANES)),
        vmem((2, 2, EDGE, LANES)),
        vmem((2, 2, EDGE, LANES)),
    ] * 2
    in_vmem = pl.BlockSpec(memory_space=pltpu.VMEM)
    ending = pl.pallas_call(
        functools.partial(kernel, sizes, levels, rows, cols),
        out_shape=pltpu.VMEM((levels * rows, cols), jnp.float32),
        in_specs=[pl.BlockSpec(memory_space=pl.ANY), in_vmem, in_vmem],
        out_specs=in_vmem,
        scratch_shapes=scratch,
        compiler_params=pltpu.CompilerParams(collective_id=0, has_side_effects=True),
        name="parareal",
    )(state_starts.reshape(levels * rows, cols), diffusivity.reshape(1, levels), wind)
    return ending.reshape(1, levels, rows, cols)


def solution(mesh):
    sizes = tuple(mesh.shape[axis] for axis in ("tm", "gx", "gy"))
    placed = (P("tm", None, "gx", "gy"), P(), P())
    return jax.shard_map(
        functools.partial(shards, sizes),
        mesh=mesh, in_specs=placed, out_specs=P("tm", None, "gx", "gy"), check_vma=False,
    )
```

```python
import functools

import jax
import jax.numpy as jnp
from jax import lax
from jax.experimental import pallas as pl
from jax.experimental.pallas import tpu as pltpu
from jax.sharding import PartitionSpec as P

SUB = 4
REACH = SUB
RATIO = 4
LANES = 128
EDGE = 8
FRONT = 2 * EDGE
COARSE_REACH = 2

time_step = 0.2
weights_low = (0.375, 0.125, 0.0, 0.0)
weights_mid = (0.625, 0.875, 0.875, 0.625)
weights_high = (0.0, 0.0, 0.125, 0.375)
mean_side, mean_mid = 0.125, 0.75

PLANE = tuple((dx, dy) for dx in (-1, 0, 1) for dy in (-1, 0, 1))
AROUND = tuple(d for d in PLANE if d != (0, 0))


def conjunction(conditions):
    total = True
    for condition in conditions:
        total = condition if total is True else jnp.logical_and(total, condition)
    return total


def kernel(
    sizes, levels, rows, cols,
    x_hbm, diff_ref, wind_ref, out_ref,
    x_ref, load_sem,
    first, second, x_send, x_recv, old_wide, new_wide, extended, old_image, change,
    sent, fine_mean, line, fine_line, raw_edge, spread_rows, turned,
    fine_out, fine_in, old_out, old_in, chain_out, chain_in, *strip_refs,
):
    n_tm, n_gx, n_gy = sizes
    tm, gx, gy = lax.axis_index("tm"), lax.axis_index("gx"), lax.axis_index("gy")
    packs = LANES // levels
    part = rows // packs
    part_c = part // RATIO
    cols_c = cols // RATIO
    wide = part + 2 * REACH
    wide_c = part_c + 2 * COARSE_REACH
    end = FRONT + cols
    end_c = FRONT + cols_c

    def there(dz, dx, dy):
        tests = []
        for place, move, count in ((tm, dz, n_tm), (gx, dx, n_gx), (gy, dy, n_gy)):
            if move < 0:
                tests.append(place > 0)
            if move > 0:
                tests.append(place < count - 1)
        return conjunction(tests)

    def guarded(condition, action):
        if condition is True:
            action()
        else:
            pl.when(condition)(action)

    def target(dz, dx, dy):
        return (tm + dz, gx + dx, gy + dy)

    load = pltpu.make_async_copy(x_hbm, x_ref, load_sem)
    load.start()

    barrier = pltpu.get_barrier_semaphore()
    partners = [(dz, dx, dy) for dz in (-1, 0, 1) for dx, dy in PLANE if (dz, dx, dy) != (0, 0, 0)]
    partners.sort(key=lambda move: -sum(map(abs, move)))
    awaited = jnp.int32(0)
    for move in partners:
        def greet(move=move):
            pl.semaphore_signal(barrier, inc=1, device_id=target(*move), device_id_type=pl.DeviceIdType.MESH)
        guarded(there(*move), greet)
        awaited = awaited + there(*move).astype(jnp.int32)

    def send_all(copies, dz, moves):
        for move in moves:
            guarded(there(dz, *move), lambda move=move: copies[move].start())

    def sends_done(copies, dz, moves):
        for move in moves:
            guarded(there(dz, *move), lambda move=move: copies[move].wait_send())

    def all_arrived(copies, dz, moves):
        for dx, dy in moves:
            guarded(there(-dz, -dx, -dy), lambda move=(dx, dy): copies[move].wait_recv())

    def remote(source, landing, out_sem, in_sem, move):
        return pltpu.make_async_remote_copy(
            src_ref=source, dst_ref=landing, send_sem=out_sem, recv_sem=in_sem,
            device_id=target(*move), device_id_type=pl.DeviceIdType.MESH,
        )

    def index_of(move):
        return (move[0] + 1) * 3 + move[1] + 1

    fine_copies = {}
    for move in AROUND:
        dx, dy = move
        k = index_of(move)
        if dy == 0:
            source, landing = x_send.at[(dx + 1) // 2], x_recv.at[(dx + 1) // 2]
        else:
            take_row, put_row, height = {
                0: (REACH, REACH, part), -1: (REACH, REACH + part, REACH), 1: (part, 0, REACH)
            }[dx]
            take, put = {-1: (FRONT, end), 1: (end - EDGE, FRONT - EDGE)}[dy]
            source = first.at[pl.ds(take_row, height), pl.ds(take, EDGE)]
            landing = first.at[pl.ds(put_row, height), pl.ds(put, EDGE)]
        fine_copies[move] = remote(source, landing, fine_out.at[k], fine_in.at[k], (0, dx, dy))

    def coarse_copies(main, wide_in, strips, out_sems, in_sems, dz):
        row_out, row_in, side_out, side_in, corner_out, corner_in = strips
        copies = {}
        for dx, dy in PLANE if dz else AROUND:
            k = index_of((dx, dy))
            towards_x, towards_y = (dx + 1) // 2, (dy + 1) // 2
            if dx == 0 and dy == 0:
                source, landing = main, wide_in.at[pl.ds(COARSE_REACH, part_c), pl.ds(FRONT, cols_c)]
            elif dy == 0:
                source, landing = row_out.at[towards_x], row_in.at[towards_x, pl.ds(FRONT, cols_c)]
            elif dx == 0:
                source, landing = side_out.at[towards_y], side_in.at[towards_y]
            else:
                source, landing = corner_out.at[towards_x, towards_y], corner_in.at[towards_x, towards_y]
            copies[dx, dy] = remote(source, landing, out_sems.at[k], in_sems.at[k], (dz, dx, dy))
        return copies

    old_strips, new_strips = strip_refs[:6], strip_refs[6:]
    old_copies = coarse_copies(None, old_wide, old_strips, old_out, old_in, 0)
    chain_copies = coarse_copies(sent, new_wide, new_strips, chain_out, chain_in, 1)

    lane = lax.broadcasted_iota(jnp.int32, (1, LANES), 1)
    pack = lane // levels

    def packed(row):
        return jnp.concatenate([row] * packs, axis=1)

    diffuse = packed(diff_ref[...])
    east_wind = packed(wind_ref[0:1, :])
    north_wind = packed(wind_ref[1:2, :])

    def constants(factor):
        spread = (time_step * factor) * diffuse
        return 1.0 - 4.0 * spread, spread, (0.5 * time_step) * east_wind, (0.5 * time_step) * north_wind

    fine_constants = constants(1.0)
    coarse_constants = constants(0.25)

    def advance(source, row, start, count, consts):
        keep, spread, along_x, along_y = consts
        centre = source[row, pl.ds(start, count), :]
        east = source[row + 1, pl.ds(start, count), :]
        west = source[row - 1, pl.ds(start, count), :]
        north = source[row, pl.ds(start + 1, count), :]
        south = source[row, pl.ds(start - 1, count), :]
        pushed = along_x * (east - west) + along_y * (north - south)
        return centre * (keep - pushed) + spread * ((east + west) + (north + south))

    def native_row(x):
        if x < 0:
            return x_recv[1, x + REACH]
        if x >= rows:
            return x_recv[0, x - rows]
        return x_ref[pl.ds(x, levels, stride=rows), :]

    def bring_in(row):
        stacked = jnp.concatenate([native_row(p * part + row - REACH) for p in range(packs)], axis=0)
        first[row, pl.ds(FRONT, cols), :] = stacked.T

    load.wait()
    for r in range(REACH):
        x_send[0, r] = native_row(r)
        x_send[1, r] = native_row(rows - REACH + r)
    x_moves = tuple(m for m in AROUND if m[1] == 0)
    y_moves = tuple(m for m in AROUND if m[1] != 0)
    low_lanes = lane < levels
    high_lanes = lane >= LANES - levels
    for row in range(REACH, REACH + part):
        bring_in(row)

    def restricted(source, row):
        total = source[REACH + row * RATIO, pl.ds(FRONT, cols), :]
        for r in range(1, RATIO):
            total = total + source[REACH + row * RATIO + r, pl.ds(FRONT, cols), :]
        fine_line[...] = total
        mean = fine_line[pl.ds(0, cols_c, stride=RATIO), :]
        for o in range(1, RATIO):
            mean = mean + fine_line[pl.ds(o, cols_c, stride=RATIO), :]
        return mean * (1.0 / RATIO**2)

    def swapped(value):
        return pltpu.roll(value, levels, 1)

    def pack_strips(row_of, strips):
        row_out, _, side_out, _, corner_out, _ = strips
        row_out[0] = jnp.where(low_lanes, row_of(0, 0, cols_c), swapped(row_of(1, 0, cols_c)))
        row_out[1] = jnp.where(low_lanes, swapped(row_of(part_c - 2, 0, cols_c)), row_of(part_c - 1, 0, cols_c))
        for side, col in ((0, 0), (1, cols_c - COARSE_REACH)):
            for row in range(part_c):
                side_out[side, pl.ds(COARSE_REACH * row, COARSE_REACH), :] = row_of(row, col, COARSE_REACH)
            for towards in range(2):
                corner_out[towards, side, pl.ds(0, COARSE_REACH), :] = row_out[towards, pl.ds(col, COARSE_REACH), :]

    def old_row(row, col, count):
        return old_wide[COARSE_REACH + row, pl.ds(FRONT + col, count), :]

    for row in range(part_c):
        old_wide[COARSE_REACH + row, pl.ds(FRONT, cols_c), :] = restricted(first, row)
    pack_strips(old_row, old_strips)
    pl.semaphore_wait(barrier, awaited)
    send_all(fine_copies, 0, y_moves)
    send_all(fine_copies, 0, x_moves)
    send_all(old_copies, 0, AROUND)

    def inside_x(row, reach, length):
        place = (gx * packs + pack) * length + (row - reach)
        return jnp.logical_and(place >= 0, place < n_gx * packs * length)

    def inside_y(start, count, length):
        place = gy * length + (start - FRONT) + lax.broadcasted_iota(jnp.int32, (count, LANES), 0)
        return jnp.logical_and(place >= 0, place < n_gy * length)

    side_moves = tuple(m for m in AROUND if m[0] == 0)
    corner_moves = tuple(m for m in y_moves if m[0] != 0)
    edges = ((FRONT - EDGE, inside_y(FRONT - EDGE, EDGE, cols)), (end, inside_y(end, EDGE, cols)))
    halo_rows = [*range(REACH), *range(REACH + part, wide)]
    half = cols // 2

    def update(source, dest, row, consts, last):
        for start, count in ((FRONT, half), (FRONT + half, cols - half)):
            dest[row, pl.ds(start, count), :] = advance(source, row, start, count, consts)
        if not last:
            for start, mask in edges:
                value = advance(source, row, start, EDGE, consts)
                dest[row, pl.ds(start, EDGE), :] = jnp.where(mask, value, 0.0)

    buffers = (first, second)

    all_arrived(fine_copies, 0, side_moves)
    def edge_of(start):
        return 0 if start < FRONT else 1

    for start, mask in edges:
        for row in [*range(REACH), *range(part - REACH, part)]:
            raw_edge[edge_of(start), row] = first[row + REACH, pl.ds(start, EDGE), :]
        for row in range(REACH, REACH + part):
            first[row, pl.ds(start, EDGE), :] = jnp.where(mask, first[row, pl.ds(start, EDGE), :], 0.0)
    for step in range(1, SUB + 1):
        def inner_row(row, step=step):
            update(buffers[(step - 1) % 2], buffers[step % 2], row, fine_constants, step == SUB)

        sends_done(fine_copies, 0, y_moves) if step == 2 else None
        pl.loop(REACH + step, REACH + part - step, unroll=2)(inner_row)

    all_arrived(fine_copies, 0, x_moves)
    for row in halo_rows:
        bring_in(row)
        inner = first[row, pl.ds(FRONT, cols), :]
        first[row, pl.ds(FRONT, cols), :] = jnp.where(inside_x(row, REACH, part), inner, 0.0)
    all_arrived(fine_copies, 0, corner_moves)
    for start, mask_y in edges:
        for row in halo_rows:
            here = first[row, pl.ds(start, EDGE), :]
            if row < REACH:
                here = pltpu.roll(jnp.where(high_lanes, here, raw_edge[edge_of(start), row + part - REACH]), levels, 1)
            else:
                here = pltpu.roll(jnp.where(low_lanes, here, raw_edge[edge_of(start), row - part - REACH]), LANES - levels, 1)
            mask = jnp.logical_and(mask_y, inside_x(row, REACH, part))
            first[row, pl.ds(start, EDGE), :] = jnp.where(mask, here, 0.0)
    for step in range(1, SUB + 1):
        def outer_row(row, step=step):
            for shifted in (row, row + part + REACH - 2 * step):
                mask_x = inside_x(shifted, REACH, part)
                consts = tuple(jnp.where(mask_x, c, 0.0) for c in fine_constants)
                update(buffers[(step - 1) % 2], buffers[step % 2], shifted, consts, step == SUB)

        pl.loop(step, REACH + step)(outer_row)
    sends_done(fine_copies, 0, x_moves)
    fine = buffers[SUB % 2]

    for row in range(part_c):
        fine_mean[row] = restricted(fine, row)

    count_c = cols_c + 2 * EDGE
    begin_c = FRONT - EDGE
    mask_y = inside_y(begin_c, count_c, cols_c)

    def extend(buffer, strips):
        _, row_in, _, side_in, _, corner_in = strips
        for side, col in ((0, end_c), (1, FRONT - COARSE_REACH)):
            for row in range(part_c):
                buffer[COARSE_REACH + row, pl.ds(col, COARSE_REACH), :] = side_in[
                    side, pl.ds(COARSE_REACH * row, COARSE_REACH), :
                ]
            for towards in range(2):
                row_in[towards, pl.ds(col, COARSE_REACH), :] = corner_in[towards, side, pl.ds(0, COARSE_REACH), :]

        def own(row):
            return buffer[COARSE_REACH + row, pl.ds(begin_c, count_c), :]

        above, below = (row_in[towards, pl.ds(begin_c, count_c), :] for towards in (0, 1))
        values = [
            jnp.where(low_lanes, below, swapped(own(part_c - 2))),
            swapped(jnp.where(high_lanes, below, own(part_c - 1))),
            *[own(row) for row in range(part_c)],
            swapped(jnp.where(low_lanes, above, own(0))),
            jnp.where(high_lanes, above, swapped(own(1))),
        ]
        for row, value in enumerate(values):
            mask = mask_y
            if not COARSE_REACH <= row < COARSE_REACH + part_c:
                mask = jnp.logical_and(mask_y, inside_x(row, COARSE_REACH, part_c))
            extended[row, pl.ds(begin_c, count_c), :] = jnp.where(mask, value, 0.0)

    all_arrived(old_copies, 0, AROUND)
    sends_done(old_copies, 0, AROUND)
    extend(old_wide, old_strips)
    for row in range(1, wide_c - 1):
        old_image[row - 1] = advance(extended, row, begin_c, count_c, coarse_constants)

    def write_fine():
        for row in range(part):
            turned[row] = fine[REACH + row, pl.ds(FRONT, cols), :].T

    @pl.when(tm > 0)
    def _():
        write_fine()
        all_arrived(chain_copies, 1, PLANE)
        extend(new_wide, new_strips)

    for row in range(1, wide_c - 1):
        moved = advance(extended, row, begin_c, count_c, coarse_constants) - old_image[row - 1]
        mask = jnp.logical_and(mask_y, inside_x(row, COARSE_REACH, part_c))
        change[row - 1, pl.ds(begin_c, count_c), :] = jnp.where(mask, moved, 0.0)

    def change_row(row):
        return change[row, pl.ds(begin_c, count_c), :]

    @pl.when(tm < n_tm - 1)
    def _():
        for row in range(part_c):
            line[pl.ds(begin_c, count_c), :] = (
                mean_side * (change_row(row) + change_row(row + 2)) + mean_mid * change_row(row + 1)
            )
            sides = line[pl.ds(FRONT - 1, cols_c), :] + line[pl.ds(FRONT + 1, cols_c), :]
            sent[row] = fine_mean[row] + mean_side * sides + mean_mid * line[pl.ds(FRONT, cols_c), :]
        pack_strips(lambda row, col, count: sent[row, pl.ds(col, count), :], new_strips)
        send_all(chain_copies, 1, AROUND)
        send_all(chain_copies, 1, ((0, 0),))

    pl.when(tm == 0)(write_fine)

    coarse_col = lax.broadcasted_iota(jnp.int32, (count_c, cols), 0) - EDGE
    fine_col = lax.broadcasted_iota(jnp.int32, (count_c, cols), 1)
    offset_of = fine_col & (RATIO - 1)
    apart = coarse_col - (fine_col >> (RATIO.bit_length() - 1))
    spreading = jnp.zeros((count_c, cols), jnp.float32)
    for o in range(RATIO):
        for distance, weights in ((-1, weights_low), (0, weights_mid), (1, weights_high)):
            chosen = jnp.logical_and(offset_of == o, apart == distance)
            spreading = jnp.where(chosen, weights[o], spreading)
    spreading = jnp.concatenate([spreading.astype(jnp.bfloat16)] * 3, axis=0)
    for row in range(part_c + 2):
        rest, pieces = change_row(row), []
        for _ in range(3):
            piece = rest.astype(jnp.bfloat16).astype(jnp.float32)
            pieces.append(piece)
            rest = rest - piece
        split = jnp.concatenate(pieces, axis=0).T.astype(jnp.bfloat16)
        spread_rows[row] = jnp.dot(split, spreading, preferred_element_type=jnp.float32)

    for row in range(part):
        at, o = row // RATIO, row % RATIO
        total = turned[row] + weights_mid[o] * spread_rows[at + 1]
        if weights_low[o]:
            total = total + weights_low[o] * spread_rows[at]
        if weights_high[o]:
            total = total + weights_high[o] * spread_rows[at + 2]
        for p in range(packs):
            out_ref[pl.ds(p * part + row, levels, stride=rows), :] = total[p * levels : (p + 1) * levels]

    pl.when(tm < n_tm - 1)(lambda: sends_done(chain_copies, 1, PLANE))


def shards(sizes, state_starts, diffusivity, wind):
    _, levels, rows, cols = state_starts.shape
    packs = LANES // levels
    if packs != 2 or levels * packs != LANES:
        raise ValueError(levels)
    part = rows // packs
    part_c = part // RATIO
    cols_c = cols // RATIO
    wide, wide_c = part + 2 * REACH, part_c + 2 * COARSE_REACH
    vmem = functools.partial(pltpu.VMEM, dtype=jnp.float32)
    scratch = [
        vmem((levels * rows, cols)),
        pltpu.SemaphoreType.DMA,
        vmem((wide, cols + 2 * FRONT, LANES)),
        vmem((wide, cols + 2 * FRONT, LANES)),
        vmem((2, REACH, levels, cols)),
        vmem((2, REACH, levels, cols)),
        vmem((wide_c, cols_c + 2 * FRONT, LANES)),
        vmem((wide_c, cols_c + 2 * FRONT, LANES)),
        vmem((wide_c, cols_c + 2 * FRONT, LANES)),
        vmem((wide_c - 2, cols_c + 2 * EDGE, LANES)),
        vmem((wide_c - 2, cols_c + 2 * FRONT, LANES)),
        vmem((part_c, cols_c, LANES)),
        vmem((part_c, cols_c, LANES)),
        vmem((cols_c + 2 * FRONT, LANES)),
        vmem((cols, LANES)),
        vmem((2, part, EDGE, LANES)),
        vmem((part_c + 2, LANES, cols)),
        vmem((part, LANES, cols)),
    ] + [pltpu.SemaphoreType.DMA((9,))] * 6
    scratch += [
        vmem((2, cols_c, LANES)),
        vmem((2, cols_c + 2 * FRONT, LANES)),
        vmem((2, COARSE_REACH * part_c, LANES)),
        vmem((2, COARSE_REACH * part_c, LANES)),
        vmem((2, 2, EDGE, LANES)),
        vmem((2, 2, EDGE, LANES)),
    ] * 2
    in_vmem = pl.BlockSpec(memory_space=pltpu.VMEM)
    ending = pl.pallas_call(
        functools.partial(kernel, sizes, levels, rows, cols),
        out_shape=pltpu.VMEM((levels * rows, cols), jnp.float32),
        in_specs=[pl.BlockSpec(memory_space=pl.ANY), in_vmem, in_vmem],
        out_specs=in_vmem,
        scratch_shapes=scratch,
        compiler_params=pltpu.CompilerParams(collective_id=0, has_side_effects=True),
        name="parareal",
    )(state_starts.reshape(levels * rows, cols), diffusivity.reshape(1, levels), wind)
    return ending.reshape(1, levels, rows, cols)


def solution(mesh):
    sizes = tuple(mesh.shape[axis] for axis in ("tm", "gx", "gy"))
    placed = (P("tm", None, "gx", "gy"), P(), P())
    return jax.shard_map(
        functools.partial(shards, sizes),
        mesh=mesh, in_specs=placed, out_specs=P("tm", None, "gx", "gy"), check_vma=False,
    )
```

```python
import functools

import jax
import jax.numpy as jnp
from jax import lax
from jax.experimental import pallas as pl
from jax.experimental.pallas import tpu as pltpu
from jax.sharding import PartitionSpec as P

SUB = 4
REACH = SUB
RATIO = 4
LANES = 128
EDGE = 8
FRONT = 2 * EDGE
COARSE_REACH = 2

time_step = 0.2
weights_low = (0.375, 0.125, 0.0, 0.0)
weights_mid = (0.625, 0.875, 0.875, 0.625)
weights_high = (0.0, 0.0, 0.125, 0.375)
mean_side, mean_mid = 0.125, 0.75

PLANE = tuple((dx, dy) for dx in (-1, 0, 1) for dy in (-1, 0, 1))
AROUND = tuple(d for d in PLANE if d != (0, 0))


def conjunction(conditions):
    total = True
    for condition in conditions:
        total = condition if total is True else jnp.logical_and(total, condition)
    return total


def kernel(
    sizes, levels, rows, cols,
    x_hbm, diff_ref, wind_ref, out_ref,
    x_ref, load_sem,
    first, second, x_recv, old_wide, new_wide, extended, old_image, change,
    sent, fine_mean, line, fine_line, raw_edge, spread_rows, turned,
    fine_out, fine_in, old_out, old_in, chain_out, chain_in, *strip_refs,
):
    n_tm, n_gx, n_gy = sizes
    tm, gx, gy = lax.axis_index("tm"), lax.axis_index("gx"), lax.axis_index("gy")
    packs = LANES // levels
    part = rows // packs
    part_c = part // RATIO
    cols_c = cols // RATIO
    wide = part + 2 * REACH
    wide_c = part_c + 2 * COARSE_REACH
    end = FRONT + cols
    end_c = FRONT + cols_c

    def there(dz, dx, dy):
        tests = []
        for place, move, count in ((tm, dz, n_tm), (gx, dx, n_gx), (gy, dy, n_gy)):
            if move < 0:
                tests.append(place > 0)
            if move > 0:
                tests.append(place < count - 1)
        return conjunction(tests)

    def guarded(condition, action):
        if condition is True:
            action()
        else:
            pl.when(condition)(action)

    def target(dz, dx, dy):
        return (tm + dz, gx + dx, gy + dy)

    loads = [pltpu.make_async_copy(x_hbm.at[:, x], x_ref.at[x], load_sem.at[x]) for x in range(rows)]
    for x in sorted(range(rows), key=lambda x: min(x, rows - 1 - x) >= REACH):
        loads[x].start()

    barrier = pltpu.get_barrier_semaphore()
    partners = [(dz, dx, dy) for dz in (-1, 0, 1) for dx, dy in PLANE if (dz, dx, dy) != (0, 0, 0)]
    partners.sort(key=lambda move: -sum(map(abs, move)))
    awaited = jnp.int32(0)
    for move in partners:
        def greet(move=move):
            pl.semaphore_signal(barrier, inc=1, device_id=target(*move), device_id_type=pl.DeviceIdType.MESH)
        guarded(there(*move), greet)
        awaited = awaited + there(*move).astype(jnp.int32)

    def send_all(copies, dz, moves):
        for move in moves:
            guarded(there(dz, *move), lambda move=move: copies[move].start())

    def sends_done(copies, dz, moves):
        for move in moves:
            guarded(there(dz, *move), lambda move=move: copies[move].wait_send())

    def all_arrived(copies, dz, moves):
        for dx, dy in moves:
            guarded(there(-dz, -dx, -dy), lambda move=(dx, dy): copies[move].wait_recv())

    def remote(source, landing, out_sem, in_sem, move):
        return pltpu.make_async_remote_copy(
            src_ref=source, dst_ref=landing, send_sem=out_sem, recv_sem=in_sem,
            device_id=target(*move), device_id_type=pl.DeviceIdType.MESH,
        )

    def index_of(move):
        return (move[0] + 1) * 3 + move[1] + 1

    fine_copies = {}
    for move in AROUND:
        dx, dy = move
        k = index_of(move)
        if dy == 0:
            source, landing = x_ref.at[pl.ds((0, 0, rows - REACH)[dx + 1], REACH)], x_recv.at[(dx + 1) // 2]
        else:
            take_row, put_row, height = {
                0: (REACH, REACH, part), -1: (REACH, REACH + part, REACH), 1: (part, 0, REACH)
            }[dx]
            take, put = {-1: (FRONT, end), 1: (end - EDGE, FRONT - EDGE)}[dy]
            source = first.at[pl.ds(take_row, height), pl.ds(take, EDGE)]
            landing = first.at[pl.ds(put_row, height), pl.ds(put, EDGE)]
        fine_copies[move] = remote(source, landing, fine_out.at[k], fine_in.at[k], (0, dx, dy))

    def coarse_copies(main, wide_in, strips, out_sems, in_sems, dz):
        row_out, row_in, side_out, side_in, corner_out, corner_in = strips
        copies = {}
        for dx, dy in PLANE if dz else AROUND:
            k = index_of((dx, dy))
            towards_x, towards_y = (dx + 1) // 2, (dy + 1) // 2
            if dx == 0 and dy == 0:
                source, landing = main, wide_in.at[pl.ds(COARSE_REACH, part_c), pl.ds(FRONT, cols_c)]
            elif dy == 0:
                source, landing = row_out.at[towards_x], row_in.at[towards_x, pl.ds(FRONT, cols_c)]
            elif dx == 0:
                source, landing = side_out.at[towards_y], side_in.at[towards_y]
            else:
                source, landing = corner_out.at[towards_x, towards_y], corner_in.at[towards_x, towards_y]
            copies[dx, dy] = remote(source, landing, out_sems.at[k], in_sems.at[k], (dz, dx, dy))
        return copies

    old_strips, new_strips = strip_refs[:6], strip_refs[6:]
    old_copies = coarse_copies(None, old_wide, old_strips, old_out, old_in, 0)
    chain_copies = coarse_copies(sent, new_wide, new_strips, chain_out, chain_in, 1)

    lane = lax.broadcasted_iota(jnp.int32, (1, LANES), 1)
    pack = lane // levels

    def packed(row):
        return jnp.concatenate([row] * packs, axis=1)

    diffuse = packed(diff_ref[...])
    east_wind = packed(wind_ref[0:1, :])
    north_wind = packed(wind_ref[1:2, :])

    def constants(factor):
        spread = (time_step * factor) * diffuse
        return 1.0 - 4.0 * spread, spread, (0.5 * time_step) * east_wind, (0.5 * time_step) * north_wind

    fine_constants = constants(1.0)
    coarse_constants = constants(0.25)

    def advance(source, row, start, count, consts):
        keep, spread, along_x, along_y = consts
        centre = source[row, pl.ds(start, count), :]
        east = source[row + 1, pl.ds(start, count), :]
        west = source[row - 1, pl.ds(start, count), :]
        north = source[row, pl.ds(start + 1, count), :]
        south = source[row, pl.ds(start - 1, count), :]
        pushed = along_x * (east - west) + along_y * (north - south)
        return centre * (keep - pushed) + spread * ((east + west) + (north + south))

    def native_row(x):
        if x < 0:
            return x_recv[1, x + REACH]
        if x >= rows:
            return x_recv[0, x - rows]
        return x_ref[x]

    def bring_in(row):
        stacked = jnp.concatenate([native_row(p * part + row - REACH) for p in range(packs)], axis=0)
        first[row, pl.ds(FRONT, cols), :] = stacked.T

    for load in loads:
        load.wait()
    x_moves = tuple(m for m in AROUND if m[1] == 0)
    y_moves = tuple(m for m in AROUND if m[1] != 0)
    low_lanes = lane < levels
    high_lanes = lane >= LANES - levels
    for row in range(REACH, REACH + part):
        bring_in(row)

    def restricted(source, row):
        total = source[REACH + row * RATIO, pl.ds(FRONT, cols), :]
        for r in range(1, RATIO):
            total = total + source[REACH + row * RATIO + r, pl.ds(FRONT, cols), :]
        fine_line[...] = total
        mean = fine_line[pl.ds(0, cols_c, stride=RATIO), :]
        for o in range(1, RATIO):
            mean = mean + fine_line[pl.ds(o, cols_c, stride=RATIO), :]
        return mean * (1.0 / RATIO**2)

    def swapped(value):
        return pltpu.roll(value, levels, 1)

    def pack_strips(row_of, strips):
        row_out, _, side_out, _, corner_out, _ = strips
        row_out[0] = jnp.where(low_lanes, row_of(0, 0, cols_c), swapped(row_of(1, 0, cols_c)))
        row_out[1] = jnp.where(low_lanes, swapped(row_of(part_c - 2, 0, cols_c)), row_of(part_c - 1, 0, cols_c))
        for side, col in ((0, 0), (1, cols_c - COARSE_REACH)):
            for row in range(part_c):
                side_out[side, pl.ds(COARSE_REACH * row, COARSE_REACH), :] = row_of(row, col, COARSE_REACH)
            for towards in range(2):
                corner_out[towards, side, pl.ds(0, COARSE_REACH), :] = row_out[towards, pl.ds(col, COARSE_REACH), :]

    def old_row(row, col, count):
        return old_wide[COARSE_REACH + row, pl.ds(FRONT + col, count), :]

    for row in range(part_c):
        old_wide[COARSE_REACH + row, pl.ds(FRONT, cols_c), :] = restricted(first, row)
    pack_strips(old_row, old_strips)
    pl.semaphore_wait(barrier, awaited)
    send_all(fine_copies, 0, x_moves)
    send_all(fine_copies, 0, y_moves)
    send_all(old_copies, 0, AROUND)

    def inside_x(row, reach, length):
        place = (gx * packs + pack) * length + (row - reach)
        return jnp.logical_and(place >= 0, place < n_gx * packs * length)

    def inside_y(start, count, length):
        place = gy * length + (start - FRONT) + lax.broadcasted_iota(jnp.int32, (count, LANES), 0)
        return jnp.logical_and(place >= 0, place < n_gy * length)

    side_moves = tuple(m for m in AROUND if m[0] == 0)
    corner_moves = tuple(m for m in y_moves if m[0] != 0)
    edges = ((FRONT - EDGE, inside_y(FRONT - EDGE, EDGE, cols)), (end, inside_y(end, EDGE, cols)))
    halo_rows = [*range(REACH), *range(REACH + part, wide)]
    half = cols // 2

    def update(source, dest, row, consts, last):
        for start, count in ((FRONT, half), (FRONT + half, cols - half)):
            dest[row, pl.ds(start, count), :] = advance(source, row, start, count, consts)
        if not last:
            for start, mask in edges:
                value = advance(source, row, start, EDGE, consts)
                dest[row, pl.ds(start, EDGE), :] = jnp.where(mask, value, 0.0)

    buffers = (first, second)

    all_arrived(fine_copies, 0, side_moves)
    def edge_of(start):
        return 0 if start < FRONT else 1

    for start, mask in edges:
        for row in [*range(REACH), *range(part - REACH, part)]:
            raw_edge[edge_of(start), row] = first[row + REACH, pl.ds(start, EDGE), :]
        for row in range(REACH, REACH + part):
            first[row, pl.ds(start, EDGE), :] = jnp.where(mask, first[row, pl.ds(start, EDGE), :], 0.0)
    for step in range(1, SUB + 1):
        def inner_row(row, step=step):
            update(buffers[(step - 1) % 2], buffers[step % 2], row, fine_constants, step == SUB)

        sends_done(fine_copies, 0, y_moves) if step == 2 else None
        pl.loop(REACH + step, REACH + part - step, unroll=2)(inner_row)

    all_arrived(fine_copies, 0, x_moves)
    for row in halo_rows:
        bring_in(row)
        inner = first[row, pl.ds(FRONT, cols), :]
        first[row, pl.ds(FRONT, cols), :] = jnp.where(inside_x(row, REACH, part), inner, 0.0)
    all_arrived(fine_copies, 0, corner_moves)
    for start, mask_y in edges:
        for row in halo_rows:
            here = first[row, pl.ds(start, EDGE), :]
            if row < REACH:
                here = pltpu.roll(jnp.where(high_lanes, here, raw_edge[edge_of(start), row + part - REACH]), levels, 1)
            else:
                here = pltpu.roll(jnp.where(low_lanes, here, raw_edge[edge_of(start), row - part - REACH]), LANES - levels, 1)
            mask = jnp.logical_and(mask_y, inside_x(row, REACH, part))
            first[row, pl.ds(start, EDGE), :] = jnp.where(mask, here, 0.0)
    for step in range(1, SUB + 1):
        def outer_row(row, step=step):
            for shifted in (row, row + part + REACH - 2 * step):
                mask_x = inside_x(shifted, REACH, part)
                consts = tuple(jnp.where(mask_x, c, 0.0) for c in fine_constants)
                update(buffers[(step - 1) % 2], buffers[step % 2], shifted, consts, step == SUB)

        pl.loop(step, REACH + step)(outer_row)
    sends_done(fine_copies, 0, x_moves)
    fine = buffers[SUB % 2]

    for row in range(part_c):
        fine_mean[row] = restricted(fine, row)

    count_c = cols_c + 2 * EDGE
    begin_c = FRONT - EDGE
    mask_y = inside_y(begin_c, count_c, cols_c)

    def extend(buffer, strips):
        _, row_in, _, side_in, _, corner_in = strips
        for side, col in ((0, end_c), (1, FRONT - COARSE_REACH)):
            for row in range(part_c):
                buffer[COARSE_REACH + row, pl.ds(col, COARSE_REACH), :] = side_in[
                    side, pl.ds(COARSE_REACH * row, COARSE_REACH), :
                ]
            for towards in range(2):
                row_in[towards, pl.ds(col, COARSE_REACH), :] = corner_in[towards, side, pl.ds(0, COARSE_REACH), :]

        def own(row):
            return buffer[COARSE_REACH + row, pl.ds(begin_c, count_c), :]

        above, below = (row_in[towards, pl.ds(begin_c, count_c), :] for towards in (0, 1))
        values = [
            jnp.where(low_lanes, below, swapped(own(part_c - 2))),
            swapped(jnp.where(high_lanes, below, own(part_c - 1))),
            *[own(row) for row in range(part_c)],
            swapped(jnp.where(low_lanes, above, own(0))),
            jnp.where(high_lanes, above, swapped(own(1))),
        ]
        for row, value in enumerate(values):
            mask = mask_y
            if not COARSE_REACH <= row < COARSE_REACH + part_c:
                mask = jnp.logical_and(mask_y, inside_x(row, COARSE_REACH, part_c))
            extended[row, pl.ds(begin_c, count_c), :] = jnp.where(mask, value, 0.0)

    all_arrived(old_copies, 0, AROUND)
    sends_done(old_copies, 0, AROUND)
    extend(old_wide, old_strips)
    for row in range(1, wide_c - 1):
        old_image[row - 1] = advance(extended, row, begin_c, count_c, coarse_constants)

    def write_fine():
        for row in range(part):
            turned[row] = fine[REACH + row, pl.ds(FRONT, cols), :].T

    @pl.when(tm > 0)
    def _():
        write_fine()
        all_arrived(chain_copies, 1, PLANE)
        extend(new_wide, new_strips)

    for row in range(1, wide_c - 1):
        moved = advance(extended, row, begin_c, count_c, coarse_constants) - old_image[row - 1]
        mask = jnp.logical_and(mask_y, inside_x(row, COARSE_REACH, part_c))
        change[row - 1, pl.ds(begin_c, count_c), :] = jnp.where(mask, moved, 0.0)

    def change_row(row):
        return change[row, pl.ds(begin_c, count_c), :]

    @pl.when(tm < n_tm - 1)
    def _():
        for row in range(part_c):
            line[pl.ds(begin_c, count_c), :] = (
                mean_side * (change_row(row) + change_row(row + 2)) + mean_mid * change_row(row + 1)
            )
            sides = line[pl.ds(FRONT - 1, cols_c), :] + line[pl.ds(FRONT + 1, cols_c), :]
            sent[row] = fine_mean[row] + mean_side * sides + mean_mid * line[pl.ds(FRONT, cols_c), :]
        pack_strips(lambda row, col, count: sent[row, pl.ds(col, count), :], new_strips)
        send_all(chain_copies, 1, AROUND)
        send_all(chain_copies, 1, ((0, 0),))

    pl.when(tm == 0)(write_fine)

    coarse_col = lax.broadcasted_iota(jnp.int32, (count_c, cols), 0) - EDGE
    fine_col = lax.broadcasted_iota(jnp.int32, (count_c, cols), 1)
    offset_of = fine_col & (RATIO - 1)
    apart = coarse_col - (fine_col >> (RATIO.bit_length() - 1))
    spreading = jnp.zeros((count_c, cols), jnp.float32)
    for o in range(RATIO):
        for distance, weights in ((-1, weights_low), (0, weights_mid), (1, weights_high)):
            chosen = jnp.logical_and(offset_of == o, apart == distance)
            spreading = jnp.where(chosen, weights[o], spreading)
    spreading = jnp.concatenate([spreading.astype(jnp.bfloat16)] * 3, axis=0)
    for row in range(part_c + 2):
        rest, pieces = change_row(row), []
        for _ in range(3):
            piece = rest.astype(jnp.bfloat16).astype(jnp.float32)
            pieces.append(piece)
            rest = rest - piece
        split = jnp.concatenate(pieces, axis=0).T.astype(jnp.bfloat16)
        spread_rows[row] = jnp.dot(split, spreading, preferred_element_type=jnp.float32)

    for row in range(part):
        at, o = row // RATIO, row % RATIO
        total = turned[row] + weights_mid[o] * spread_rows[at + 1]
        if weights_low[o]:
            total = total + weights_low[o] * spread_rows[at]
        if weights_high[o]:
            total = total + weights_high[o] * spread_rows[at + 2]
        for p in range(packs):
            out_ref[pl.ds(p * part + row, levels, stride=rows), :] = total[p * levels : (p + 1) * levels]

    pl.when(tm < n_tm - 1)(lambda: sends_done(chain_copies, 1, PLANE))


def shards(sizes, state_starts, diffusivity, wind):
    _, levels, rows, cols = state_starts.shape
    packs = LANES // levels
    if packs != 2 or levels * packs != LANES:
        raise ValueError(levels)
    part = rows // packs
    part_c = part // RATIO
    cols_c = cols // RATIO
    wide, wide_c = part + 2 * REACH, part_c + 2 * COARSE_REACH
    vmem = functools.partial(pltpu.VMEM, dtype=jnp.float32)
    scratch = [
        vmem((rows, levels, cols)),
        pltpu.SemaphoreType.DMA((rows,)),
        vmem((wide, cols + 2 * FRONT, LANES)),
        vmem((wide, cols + 2 * FRONT, LANES)),
        vmem((2, REACH, levels, cols)),
        vmem((wide_c, cols_c + 2 * FRONT, LANES)),
        vmem((wide_c, cols_c + 2 * FRONT, LANES)),
        vmem((wide_c, cols_c + 2 * FRONT, LANES)),
        vmem((wide_c - 2, cols_c + 2 * EDGE, LANES)),
        vmem((wide_c - 2, cols_c + 2 * FRONT, LANES)),
        vmem((part_c, cols_c, LANES)),
        vmem((part_c, cols_c, LANES)),
        vmem((cols_c + 2 * FRONT, LANES)),
        vmem((cols, LANES)),
        vmem((2, part, EDGE, LANES)),
        vmem((part_c + 2, LANES, cols)),
        vmem((part, LANES, cols)),
    ] + [pltpu.SemaphoreType.DMA((9,))] * 6
    scratch += [
        vmem((2, cols_c, LANES)),
        vmem((2, cols_c + 2 * FRONT, LANES)),
        vmem((2, COARSE_REACH * part_c, LANES)),
        vmem((2, COARSE_REACH * part_c, LANES)),
        vmem((2, 2, EDGE, LANES)),
        vmem((2, 2, EDGE, LANES)),
    ] * 2
    in_vmem = pl.BlockSpec(memory_space=pltpu.VMEM)
    ending = pl.pallas_call(
        functools.partial(kernel, sizes, levels, rows, cols),
        out_shape=pltpu.VMEM((levels * rows, cols), jnp.float32),
        in_specs=[pl.BlockSpec(memory_space=pl.ANY), in_vmem, in_vmem],
        out_specs=in_vmem,
        scratch_shapes=scratch,
        compiler_params=pltpu.CompilerParams(collective_id=0, has_side_effects=True),
        name="parareal",
    )(state_starts[0], diffusivity.reshape(1, levels), wind)
    return ending.reshape(1, levels, rows, cols)


def solution(mesh):
    sizes = tuple(mesh.shape[axis] for axis in ("tm", "gx", "gy"))
    placed = (P("tm", None, "gx", "gy"), P(), P())
    return jax.shard_map(
        functools.partial(shards, sizes),
        mesh=mesh, in_specs=placed, out_specs=P("tm", None, "gx", "gy"), check_vma=False,
    )
```

```python
import functools

import jax
import jax.numpy as jnp
from jax import lax
from jax.experimental import pallas as pl
from jax.experimental.pallas import tpu as pltpu
from jax.sharding import PartitionSpec as P

SUB = 4
REACH = SUB
RATIO = 4
LANES = 128
EDGE = 8
FRONT = 2 * EDGE
COARSE_REACH = 2

time_step = 0.2
weights_low = (0.375, 0.125, 0.0, 0.0)
weights_mid = (0.625, 0.875, 0.875, 0.625)
weights_high = (0.0, 0.0, 0.125, 0.375)
mean_side, mean_mid = 0.125, 0.75

PLANE = tuple((dx, dy) for dx in (-1, 0, 1) for dy in (-1, 0, 1))
AROUND = tuple(d for d in PLANE if d != (0, 0))


def conjunction(conditions):
    total = True
    for condition in conditions:
        total = condition if total is True else jnp.logical_and(total, condition)
    return total


def kernel(
    sizes, levels, rows, cols,
    x_hbm, diff_ref, wind_ref, out_ref,
    x_ref, load_sem, ready,
    first, second, x_send, x_recv, old_wide, new_wide, extended, old_image, change,
    sent, fine_mean, line, fine_line, raw_edge, spread_rows, turned,
    fine_out, fine_in, old_out, old_in, chain_out, chain_in, *strip_refs,
):
    n_tm, n_gx, n_gy = sizes
    tm, gx, gy = lax.axis_index("tm"), lax.axis_index("gx"), lax.axis_index("gy")
    packs = LANES // levels
    part = rows // packs
    part_c = part // RATIO
    cols_c = cols // RATIO
    wide = part + 2 * REACH
    wide_c = part_c + 2 * COARSE_REACH
    end = FRONT + cols
    end_c = FRONT + cols_c

    def there(dz, dx, dy):
        tests = []
        for place, move, count in ((tm, dz, n_tm), (gx, dx, n_gx), (gy, dy, n_gy)):
            if move < 0:
                tests.append(place > 0)
            if move > 0:
                tests.append(place < count - 1)
        return conjunction(tests)

    def guarded(condition, action):
        if condition is True:
            action()
        else:
            pl.when(condition)(action)

    def target(dz, dx, dy):
        return (tm + dz, gx + dx, gy + dy)

    load = pltpu.make_async_copy(x_hbm, x_ref, load_sem)
    load.start()

    barrier = pltpu.get_barrier_semaphore()
    partners = [(0, dx, dy) for dx, dy in AROUND] + [(-1, 0, 0), (1, 0, 0)]
    partners.sort(key=lambda move: -sum(map(abs, move)))
    awaited = jnp.int32(0)
    for move in partners:
        def greet(move=move):
            pl.semaphore_signal(barrier, inc=1, device_id=target(*move), device_id_type=pl.DeviceIdType.MESH)
        guarded(there(*move), greet)
        awaited = awaited + there(*move).astype(jnp.int32)

    def send_all(copies, dz, moves):
        for move in moves:
            guarded(there(dz, *move), lambda move=move: copies[move].start())

    def sends_done(copies, dz, moves):
        for move in moves:
            guarded(there(dz, *move), lambda move=move: copies[move].wait_send())

    def all_arrived(copies, dz, moves):
        for dx, dy in moves:
            guarded(there(-dz, -dx, -dy), lambda move=(dx, dy): copies[move].wait_recv())

    def remote(source, landing, out_sem, in_sem, move):
        return pltpu.make_async_remote_copy(
            src_ref=source, dst_ref=landing, send_sem=out_sem, recv_sem=in_sem,
            device_id=target(*move), device_id_type=pl.DeviceIdType.MESH,
        )

    def index_of(move):
        return (move[0] + 1) * 3 + move[1] + 1

    fine_copies = {}
    for move in AROUND:
        dx, dy = move
        k = index_of(move)
        if dy == 0:
            source, landing = x_send.at[(dx + 1) // 2], x_recv.at[(dx + 1) // 2]
        else:
            take_row, put_row, height = {
                0: (REACH, REACH, part), -1: (REACH, REACH + part, REACH), 1: (part, 0, REACH)
            }[dx]
            take, put = {-1: (FRONT, end), 1: (end - EDGE, FRONT - EDGE)}[dy]
            source = first.at[pl.ds(take_row, height), pl.ds(take, EDGE)]
            landing = first.at[pl.ds(put_row, height), pl.ds(put, EDGE)]
        fine_copies[move] = remote(source, landing, fine_out.at[k], fine_in.at[k], (0, dx, dy))

    def coarse_copies(main, wide_in, strips, out_sems, in_sems, dz):
        row_out, row_in, side_out, side_in, corner_out, corner_in = strips
        copies = {}
        for dx, dy in PLANE if dz else AROUND:
            k = index_of((dx, dy))
            towards_x, towards_y = (dx + 1) // 2, (dy + 1) // 2
            if dx == 0 and dy == 0:
                source, landing = main, wide_in.at[pl.ds(COARSE_REACH, part_c), pl.ds(FRONT, cols_c)]
            elif dy == 0:
                source, landing = row_out.at[towards_x], row_in.at[towards_x, pl.ds(FRONT, cols_c)]
            elif dx == 0:
                source, landing = side_out.at[towards_y], side_in.at[towards_y]
            else:
                source, landing = corner_out.at[towards_x, towards_y], corner_in.at[towards_x, towards_y]
            copies[dx, dy] = remote(source, landing, out_sems.at[k], in_sems.at[k], (dz, dx, dy))
        return copies

    old_strips, new_strips = strip_refs[:6], strip_refs[6:]
    old_copies = coarse_copies(None, old_wide, old_strips, old_out, old_in, 0)
    chain_copies = coarse_copies(sent, new_wide, new_strips, chain_out, chain_in, 1)

    lane = lax.broadcasted_iota(jnp.int32, (1, LANES), 1)
    pack = lane // levels

    def packed(row):
        return jnp.concatenate([row] * packs, axis=1)

    diffuse = packed(diff_ref[...])
    east_wind = packed(wind_ref[0:1, :])
    north_wind = packed(wind_ref[1:2, :])

    def constants(factor):
        spread = (time_step * factor) * diffuse
        return 1.0 - 4.0 * spread, spread, (0.5 * time_step) * east_wind, (0.5 * time_step) * north_wind

    fine_constants = constants(1.0)
    coarse_constants = constants(0.25)

    def advance(source, row, start, count, consts):
        keep, spread, along_x, along_y = consts
        centre = source[row, pl.ds(start, count), :]
        east = source[row + 1, pl.ds(start, count), :]
        west = source[row - 1, pl.ds(start, count), :]
        north = source[row, pl.ds(start + 1, count), :]
        south = source[row, pl.ds(start - 1, count), :]
        pushed = along_x * (east - west) + along_y * (north - south)
        return centre * (keep - pushed) + spread * ((east + west) + (north + south))

    def native_row(x):
        if x < 0:
            return x_recv[1, x + REACH]
        if x >= rows:
            return x_recv[0, x - rows]
        return x_ref[pl.ds(x, levels, stride=rows), :]

    def bring_in(row):
        stacked = jnp.concatenate([native_row(p * part + row - REACH) for p in range(packs)], axis=0)
        first[row, pl.ds(FRONT, cols), :] = stacked.T

    load.wait()
    for r in range(REACH):
        x_send[0, r] = native_row(r)
        x_send[1, r] = native_row(rows - REACH + r)
    x_moves = tuple(m for m in AROUND if m[1] == 0)
    y_moves = tuple(m for m in AROUND if m[1] != 0)
    low_lanes = lane < levels
    high_lanes = lane >= LANES - levels
    for row in range(REACH, REACH + part):
        bring_in(row)

    def restricted(source, row):
        total = source[REACH + row * RATIO, pl.ds(FRONT, cols), :]
        for r in range(1, RATIO):
            total = total + source[REACH + row * RATIO + r, pl.ds(FRONT, cols), :]
        fine_line[...] = total
        mean = fine_line[pl.ds(0, cols_c, stride=RATIO), :]
        for o in range(1, RATIO):
            mean = mean + fine_line[pl.ds(o, cols_c, stride=RATIO), :]
        return mean * (1.0 / RATIO**2)

    def swapped(value):
        return pltpu.roll(value, levels, 1)

    def pack_strips(row_of, strips):
        row_out, _, side_out, _, corner_out, _ = strips
        row_out[0] = jnp.where(low_lanes, row_of(0, 0, cols_c), swapped(row_of(1, 0, cols_c)))
        row_out[1] = jnp.where(low_lanes, swapped(row_of(part_c - 2, 0, cols_c)), row_of(part_c - 1, 0, cols_c))
        for side, col in ((0, 0), (1, cols_c - COARSE_REACH)):
            for row in range(part_c):
                side_out[side, pl.ds(COARSE_REACH * row, COARSE_REACH), :] = row_of(row, col, COARSE_REACH)
            for towards in range(2):
                corner_out[towards, side, pl.ds(0, COARSE_REACH), :] = row_out[towards, pl.ds(col, COARSE_REACH), :]

    def old_row(row, col, count):
        return old_wide[COARSE_REACH + row, pl.ds(FRONT + col, count), :]

    for row in range(part_c):
        old_wide[COARSE_REACH + row, pl.ds(FRONT, cols_c), :] = restricted(first, row)
    pack_strips(old_row, old_strips)
    pl.semaphore_wait(barrier, awaited)

    @pl.when(tm > 0)
    def _():
        pl.semaphore_signal(ready, inc=1, device_id=target(-1, 0, 0), device_id_type=pl.DeviceIdType.MESH)

    send_all(fine_copies, 0, y_moves)
    send_all(fine_copies, 0, x_moves)
    send_all(old_copies, 0, AROUND)

    def inside_x(row, reach, length):
        place = (gx * packs + pack) * length + (row - reach)
        return jnp.logical_and(place >= 0, place < n_gx * packs * length)

    def inside_y(start, count, length):
        place = gy * length + (start - FRONT) + lax.broadcasted_iota(jnp.int32, (count, LANES), 0)
        return jnp.logical_and(place >= 0, place < n_gy * length)

    side_moves = tuple(m for m in AROUND if m[0] == 0)
    corner_moves = tuple(m for m in y_moves if m[0] != 0)
    edges = ((FRONT - EDGE, inside_y(FRONT - EDGE, EDGE, cols)), (end, inside_y(end, EDGE, cols)))
    halo_rows = [*range(REACH), *range(REACH + part, wide)]
    half = cols // 2

    def update(source, dest, row, consts, last):
        for start, count in ((FRONT, half), (FRONT + half, cols - half)):
            dest[row, pl.ds(start, count), :] = advance(source, row, start, count, consts)
        if not last:
            for start, mask in edges:
                value = advance(source, row, start, EDGE, consts)
                dest[row, pl.ds(start, EDGE), :] = jnp.where(mask, value, 0.0)

    buffers = (first, second)

    all_arrived(fine_copies, 0, side_moves)
    def edge_of(start):
        return 0 if start < FRONT else 1

    for start, mask in edges:
        for row in [*range(REACH), *range(part - REACH, part)]:
            raw_edge[edge_of(start), row] = first[row + REACH, pl.ds(start, EDGE), :]
        for row in range(REACH, REACH + part):
            first[row, pl.ds(start, EDGE), :] = jnp.where(mask, first[row, pl.ds(start, EDGE), :], 0.0)
    for step in range(1, SUB + 1):
        def inner_row(row, step=step):
            update(buffers[(step - 1) % 2], buffers[step % 2], row, fine_constants, step == SUB)

        sends_done(fine_copies, 0, y_moves) if step == 2 else None
        pl.loop(REACH + step, REACH + part - step, unroll=2)(inner_row)

    all_arrived(fine_copies, 0, x_moves)
    for row in halo_rows:
        bring_in(row)
        inner = first[row, pl.ds(FRONT, cols), :]
        first[row, pl.ds(FRONT, cols), :] = jnp.where(inside_x(row, REACH, part), inner, 0.0)
    all_arrived(fine_copies, 0, corner_moves)
    for start, mask_y in edges:
        for row in halo_rows:
            here = first[row, pl.ds(start, EDGE), :]
            if row < REACH:
                here = pltpu.roll(jnp.where(high_lanes, here, raw_edge[edge_of(start), row + part - REACH]), levels, 1)
            else:
                here = pltpu.roll(jnp.where(low_lanes, here, raw_edge[edge_of(start), row - part - REACH]), LANES - levels, 1)
            mask = jnp.logical_and(mask_y, inside_x(row, REACH, part))
            first[row, pl.ds(start, EDGE), :] = jnp.where(mask, here, 0.0)
    for step in range(1, SUB + 1):
        def outer_row(row, step=step):
            for shifted in (row, row + part + REACH - 2 * step):
                mask_x = inside_x(shifted, REACH, part)
                consts = tuple(jnp.where(mask_x, c, 0.0) for c in fine_constants)
                update(buffers[(step - 1) % 2], buffers[step % 2], shifted, consts, step == SUB)

        pl.loop(step, REACH + step)(outer_row)
    sends_done(fine_copies, 0, x_moves)
    fine = buffers[SUB % 2]

    for row in range(part_c):
        fine_mean[row] = restricted(fine, row)

    count_c = cols_c + 2 * EDGE
    begin_c = FRONT - EDGE
    mask_y = inside_y(begin_c, count_c, cols_c)

    def extend(buffer, strips):
        _, row_in, _, side_in, _, corner_in = strips
        for side, col in ((0, end_c), (1, FRONT - COARSE_REACH)):
            for row in range(part_c):
                buffer[COARSE_REACH + row, pl.ds(col, COARSE_REACH), :] = side_in[
                    side, pl.ds(COARSE_REACH * row, COARSE_REACH), :
                ]
            for towards in range(2):
                row_in[towards, pl.ds(col, COARSE_REACH), :] = corner_in[towards, side, pl.ds(0, COARSE_REACH), :]

        def own(row):
            return buffer[COARSE_REACH + row, pl.ds(begin_c, count_c), :]

        above, below = (row_in[towards, pl.ds(begin_c, count_c), :] for towards in (0, 1))
        values = [
            jnp.where(low_lanes, below, swapped(own(part_c - 2))),
            swapped(jnp.where(high_lanes, below, own(part_c - 1))),
            *[own(row) for row in range(part_c)],
            swapped(jnp.where(low_lanes, above, own(0))),
            jnp.where(high_lanes, above, swapped(own(1))),
        ]
        for row, value in enumerate(values):
            mask = mask_y
            if not COARSE_REACH <= row < COARSE_REACH + part_c:
                mask = jnp.logical_and(mask_y, inside_x(row, COARSE_REACH, part_c))
            extended[row, pl.ds(begin_c, count_c), :] = jnp.where(mask, value, 0.0)

    all_arrived(old_copies, 0, AROUND)
    sends_done(old_copies, 0, AROUND)
    extend(old_wide, old_strips)
    for row in range(1, wide_c - 1):
        old_image[row - 1] = advance(extended, row, begin_c, count_c, coarse_constants)

    pl.when(tm < n_tm - 1)(lambda: pl.semaphore_wait(ready, 1))

    def write_fine():
        for row in range(part):
            turned[row] = fine[REACH + row, pl.ds(FRONT, cols), :].T

    @pl.when(tm > 0)
    def _():
        write_fine()
        all_arrived(chain_copies, 1, PLANE)
        extend(new_wide, new_strips)

    for row in range(1, wide_c - 1):
        moved = advance(extended, row, begin_c, count_c, coarse_constants) - old_image[row - 1]
        mask = jnp.logical_and(mask_y, inside_x(row, COARSE_REACH, part_c))
        change[row - 1, pl.ds(begin_c, count_c), :] = jnp.where(mask, moved, 0.0)

    def change_row(row):
        return change[row, pl.ds(begin_c, count_c), :]

    @pl.when(tm < n_tm - 1)
    def _():
        for row in range(part_c):
            line[pl.ds(begin_c, count_c), :] = (
                mean_side * (change_row(row) + change_row(row + 2)) + mean_mid * change_row(row + 1)
            )
            sides = line[pl.ds(FRONT - 1, cols_c), :] + line[pl.ds(FRONT + 1, cols_c), :]
            sent[row] = fine_mean[row] + mean_side * sides + mean_mid * line[pl.ds(FRONT, cols_c), :]
        pack_strips(lambda row, col, count: sent[row, pl.ds(col, count), :], new_strips)
        send_all(chain_copies, 1, AROUND)
        send_all(chain_copies, 1, ((0, 0),))

    pl.when(tm == 0)(write_fine)

    coarse_col = lax.broadcasted_iota(jnp.int32, (count_c, cols), 0) - EDGE
    fine_col = lax.broadcasted_iota(jnp.int32, (count_c, cols), 1)
    offset_of = fine_col & (RATIO - 1)
    apart = coarse_col - (fine_col >> (RATIO.bit_length() - 1))
    spreading = jnp.zeros((count_c, cols), jnp.float32)
    for o in range(RATIO):
        for distance, weights in ((-1, weights_low), (0, weights_mid), (1, weights_high)):
            chosen = jnp.logical_and(offset_of == o, apart == distance)
            spreading = jnp.where(chosen, weights[o], spreading)
    spreading = jnp.concatenate([spreading.astype(jnp.bfloat16)] * 3, axis=0)
    for row in range(part_c + 2):
        rest, pieces = change_row(row), []
        for _ in range(3):
            piece = rest.astype(jnp.bfloat16).astype(jnp.float32)
            pieces.append(piece)
            rest = rest - piece
        split = jnp.concatenate(pieces, axis=0).T.astype(jnp.bfloat16)
        spread_rows[row] = jnp.dot(split, spreading, preferred_element_type=jnp.float32)

    for row in range(part):
        at, o = row // RATIO, row % RATIO
        total = turned[row] + weights_mid[o] * spread_rows[at + 1]
        if weights_low[o]:
            total = total + weights_low[o] * spread_rows[at]
        if weights_high[o]:
            total = total + weights_high[o] * spread_rows[at + 2]
        for p in range(packs):
            out_ref[pl.ds(p * part + row, levels, stride=rows), :] = total[p * levels : (p + 1) * levels]

    pl.when(tm < n_tm - 1)(lambda: sends_done(chain_copies, 1, PLANE))


def shards(sizes, state_starts, diffusivity, wind):
    _, levels, rows, cols = state_starts.shape
    packs = LANES // levels
    if packs != 2 or levels * packs != LANES:
        raise ValueError(levels)
    part = rows // packs
    part_c = part // RATIO
    cols_c = cols // RATIO
    wide, wide_c = part + 2 * REACH, part_c + 2 * COARSE_REACH
    vmem = functools.partial(pltpu.VMEM, dtype=jnp.float32)
    scratch = [
        vmem((levels * rows, cols)),
        pltpu.SemaphoreType.DMA,
        pltpu.SemaphoreType.REGULAR,
        vmem((wide, cols + 2 * FRONT, LANES)),
        vmem((wide, cols + 2 * FRONT, LANES)),
        vmem((2, REACH, levels, cols)),
        vmem((2, REACH, levels, cols)),
        vmem((wide_c, cols_c + 2 * FRONT, LANES)),
        vmem((wide_c, cols_c + 2 * FRONT, LANES)),
        vmem((wide_c, cols_c + 2 * FRONT, LANES)),
        vmem((wide_c - 2, cols_c + 2 * EDGE, LANES)),
        vmem((wide_c - 2, cols_c + 2 * FRONT, LANES)),
        vmem((part_c, cols_c, LANES)),
        vmem((part_c, cols_c, LANES)),
        vmem((cols_c + 2 * FRONT, LANES)),
        vmem((cols, LANES)),
        vmem((2, part, EDGE, LANES)),
        vmem((part_c + 2, LANES, cols)),
        vmem((part, LANES, cols)),
    ] + [pltpu.SemaphoreType.DMA((9,))] * 6
    scratch += [
        vmem((2, cols_c, LANES)),
        vmem((2, cols_c + 2 * FRONT, LANES)),
        vmem((2, COARSE_REACH * part_c, LANES)),
        vmem((2, COARSE_REACH * part_c, LANES)),
        vmem((2, 2, EDGE, LANES)),
        vmem((2, 2, EDGE, LANES)),
    ] * 2
    in_vmem = pl.BlockSpec(memory_space=pltpu.VMEM)
    ending = pl.pallas_call(
        functools.partial(kernel, sizes, levels, rows, cols),
        out_shape=pltpu.VMEM((levels * rows, cols), jnp.float32),
        in_specs=[pl.BlockSpec(memory_space=pl.ANY), in_vmem, in_vmem],
        out_specs=in_vmem,
        scratch_shapes=scratch,
        compiler_params=pltpu.CompilerParams(collective_id=0, has_side_effects=True),
        name="parareal",
    )(state_starts.reshape(levels * rows, cols), diffusivity.reshape(1, levels), wind)
    return ending.reshape(1, levels, rows, cols)


def solution(mesh):
    sizes = tuple(mesh.shape[axis] for axis in ("tm", "gx", "gy"))
    placed = (P("tm", None, "gx", "gy"), P(), P())
    return jax.shard_map(
        functools.partial(shards, sizes),
        mesh=mesh, in_specs=placed, out_specs=P("tm", None, "gx", "gy"), check_vma=False,
    )
```

```python
import functools

import jax
import jax.numpy as jnp
from jax import lax
from jax.experimental import pallas as pl
from jax.experimental.pallas import tpu as pltpu
from jax.sharding import PartitionSpec as P

SUB = 4
REACH = SUB
RATIO = 4
LANES = 128
EDGE = 8
FRONT = 2 * EDGE
COARSE_REACH = 2

time_step = 0.2
weights_low = (0.375, 0.125, 0.0, 0.0)
weights_mid = (0.625, 0.875, 0.875, 0.625)
weights_high = (0.0, 0.0, 0.125, 0.375)
mean_side, mean_mid = 0.125, 0.75

PLANE = tuple((dx, dy) for dx in (-1, 0, 1) for dy in (-1, 0, 1))
AROUND = tuple(d for d in PLANE if d != (0, 0))


def conjunction(conditions):
    total = True
    for condition in conditions:
        total = condition if total is True else jnp.logical_and(total, condition)
    return total


def kernel(
    sizes, levels, rows, cols,
    x_hbm, diff_ref, wind_ref, out_ref,
    x_ref, load_sem, ready,
    first, second, x_send, x_recv, old_wide, new_wide, extended, old_image, change,
    sent, fine_mean, line, fine_line, raw_edge, spread_rows, turned,
    fine_out, fine_in, old_out, old_in, chain_out, chain_in, *strip_refs,
):
    n_tm, n_gx, n_gy = sizes
    tm, gx, gy = lax.axis_index("tm"), lax.axis_index("gx"), lax.axis_index("gy")
    packs = LANES // levels
    part = rows // packs
    part_c = part // RATIO
    cols_c = cols // RATIO
    wide = part + 2 * REACH
    wide_c = part_c + 2 * COARSE_REACH
    end = FRONT + cols
    end_c = FRONT + cols_c

    def there(dz, dx, dy):
        tests = []
        for place, move, count in ((tm, dz, n_tm), (gx, dx, n_gx), (gy, dy, n_gy)):
            if move < 0:
                tests.append(place > 0)
            if move > 0:
                tests.append(place < count - 1)
        return conjunction(tests)

    def guarded(condition, action):
        if condition is True:
            action()
        else:
            pl.when(condition)(action)

    def target(dz, dx, dy):
        return (tm + dz, gx + dx, gy + dy)

    load = pltpu.make_async_copy(x_hbm, x_ref, load_sem)
    load.start()

    barrier = pltpu.get_barrier_semaphore()
    partners = [(0, dx, dy) for dx, dy in AROUND] + [(-1, 0, 0), (1, 0, 0)]
    partners.sort(key=lambda move: -sum(map(abs, move)))
    awaited = jnp.int32(0)
    for move in partners:
        def greet(move=move):
            pl.semaphore_signal(barrier, inc=1, device_id=target(*move), device_id_type=pl.DeviceIdType.MESH)
        guarded(there(*move), greet)
        awaited = awaited + there(*move).astype(jnp.int32)

    def send_all(copies, dz, moves):
        for move in moves:
            guarded(there(dz, *move), lambda move=move: copies[move].start())

    def sends_done(copies, dz, moves):
        for move in moves:
            guarded(there(dz, *move), lambda move=move: copies[move].wait_send())

    def all_arrived(copies, dz, moves):
        for dx, dy in moves:
            guarded(there(-dz, -dx, -dy), lambda move=(dx, dy): copies[move].wait_recv())

    def remote(source, landing, out_sem, in_sem, move):
        return pltpu.make_async_remote_copy(
            src_ref=source, dst_ref=landing, send_sem=out_sem, recv_sem=in_sem,
            device_id=target(*move), device_id_type=pl.DeviceIdType.MESH,
        )

    def index_of(move):
        return (move[0] + 1) * 3 + move[1] + 1

    fine_copies = {}
    for move in AROUND:
        dx, dy = move
        k = index_of(move)
        if dy == 0:
            source, landing = x_send.at[(dx + 1) // 2], x_recv.at[(dx + 1) // 2]
        else:
            take_row, put_row, height = {
                0: (REACH, REACH, part), -1: (REACH, REACH + part, REACH), 1: (part, 0, REACH)
            }[dx]
            take, put = {-1: (FRONT, end), 1: (end - EDGE, FRONT - EDGE)}[dy]
            source = first.at[pl.ds(take_row, height), pl.ds(take, EDGE)]
            landing = first.at[pl.ds(put_row, height), pl.ds(put, EDGE)]
        fine_copies[move] = remote(source, landing, fine_out.at[k], fine_in.at[k], (0, dx, dy))

    def coarse_copies(main, wide_in, strips, out_sems, in_sems, dz):
        row_out, row_in, side_out, side_in, corner_out, corner_in = strips
        copies = {}
        for dx, dy in PLANE if dz else AROUND:
            k = index_of((dx, dy))
            towards_x, towards_y = (dx + 1) // 2, (dy + 1) // 2
            if dx == 0 and dy == 0:
                source, landing = main, wide_in.at[pl.ds(COARSE_REACH, part_c), pl.ds(FRONT, cols_c)]
            elif dy == 0:
                source, landing = row_out.at[towards_x], row_in.at[towards_x, pl.ds(FRONT, cols_c)]
            elif dx == 0:
                source, landing = side_out.at[towards_y], side_in.at[towards_y]
            else:
                source, landing = corner_out.at[towards_x, towards_y], corner_in.at[towards_x, towards_y]
            copies[dx, dy] = remote(source, landing, out_sems.at[k], in_sems.at[k], (dz, dx, dy))
        return copies

    old_strips, new_strips = strip_refs[:6], strip_refs[6:]
    old_copies = coarse_copies(None, old_wide, old_strips, old_out, old_in, 0)
    chain_copies = coarse_copies(sent, new_wide, new_strips, chain_out, chain_in, 1)

    lane = lax.broadcasted_iota(jnp.int32, (1, LANES), 1)
    pack = lane // levels

    def packed(row):
        return jnp.concatenate([row] * packs, axis=1)

    diffuse = packed(diff_ref[...])
    east_wind = packed(wind_ref[0:1, :])
    north_wind = packed(wind_ref[1:2, :])

    def constants(factor):
        spread = (time_step * factor) * diffuse
        return 1.0 - 4.0 * spread, spread, (0.5 * time_step) * east_wind, (0.5 * time_step) * north_wind

    fine_constants = constants(1.0)
    coarse_constants = constants(0.25)

    def advance(source, row, start, count, consts):
        keep, spread, along_x, along_y = consts
        centre = source[row, pl.ds(start, count), :]
        east = source[row + 1, pl.ds(start, count), :]
        west = source[row - 1, pl.ds(start, count), :]
        north = source[row, pl.ds(start + 1, count), :]
        south = source[row, pl.ds(start - 1, count), :]
        pushed = along_x * (east - west) + along_y * (north - south)
        return centre * (keep - pushed) + spread * ((east + west) + (north + south))

    def native_row(x):
        if x < 0:
            return x_recv[1, x + REACH]
        if x >= rows:
            return x_recv[0, x - rows]
        return x_ref[pl.ds(x, levels, stride=rows), :]

    def bring_in(row):
        stacked = jnp.concatenate([native_row(p * part + row - REACH) for p in range(packs)], axis=0)
        first[row, pl.ds(FRONT, cols), :] = stacked.T

    load.wait()
    for r in range(REACH):
        x_send[0, r] = native_row(r)
        x_send[1, r] = native_row(rows - REACH + r)
    x_moves = tuple(m for m in AROUND if m[1] == 0)
    y_moves = tuple(m for m in AROUND if m[1] != 0)
    low_lanes = lane < levels
    high_lanes = lane >= LANES - levels
    pl.semaphore_wait(barrier, awaited)

    @pl.when(tm > 0)
    def _():
        pl.semaphore_signal(ready, inc=1, device_id=target(-1, 0, 0), device_id_type=pl.DeviceIdType.MESH)

    send_all(fine_copies, 0, x_moves)
    for row in range(REACH, REACH + part):
        bring_in(row)
    send_all(fine_copies, 0, y_moves)

    def restricted(source, row):
        total = source[REACH + row * RATIO, pl.ds(FRONT, cols), :]
        for r in range(1, RATIO):
            total = total + source[REACH + row * RATIO + r, pl.ds(FRONT, cols), :]
        fine_line[...] = total
        mean = fine_line[pl.ds(0, cols_c, stride=RATIO), :]
        for o in range(1, RATIO):
            mean = mean + fine_line[pl.ds(o, cols_c, stride=RATIO), :]
        return mean * (1.0 / RATIO**2)

    def swapped(value):
        return pltpu.roll(value, levels, 1)

    def pack_strips(row_of, strips):
        row_out, _, side_out, _, corner_out, _ = strips
        row_out[0] = jnp.where(low_lanes, row_of(0, 0, cols_c), swapped(row_of(1, 0, cols_c)))
        row_out[1] = jnp.where(low_lanes, swapped(row_of(part_c - 2, 0, cols_c)), row_of(part_c - 1, 0, cols_c))
        for side, col in ((0, 0), (1, cols_c - COARSE_REACH)):
            for row in range(part_c):
                side_out[side, pl.ds(COARSE_REACH * row, COARSE_REACH), :] = row_of(row, col, COARSE_REACH)
            for towards in range(2):
                corner_out[towards, side, pl.ds(0, COARSE_REACH), :] = row_out[towards, pl.ds(col, COARSE_REACH), :]

    def old_row(row, col, count):
        return old_wide[COARSE_REACH + row, pl.ds(FRONT + col, count), :]

    for row in range(part_c):
        old_wide[COARSE_REACH + row, pl.ds(FRONT, cols_c), :] = restricted(first, row)
    pack_strips(old_row, old_strips)
    send_all(old_copies, 0, AROUND)

    def inside_x(row, reach, length):
        place = (gx * packs + pack) * length + (row - reach)
        return jnp.logical_and(place >= 0, place < n_gx * packs * length)

    def inside_y(start, count, length):
        place = gy * length + (start - FRONT) + lax.broadcasted_iota(jnp.int32, (count, LANES), 0)
        return jnp.logical_and(place >= 0, place < n_gy * length)

    side_moves = tuple(m for m in AROUND if m[0] == 0)
    corner_moves = tuple(m for m in y_moves if m[0] != 0)
    edges = ((FRONT - EDGE, inside_y(FRONT - EDGE, EDGE, cols)), (end, inside_y(end, EDGE, cols)))
    halo_rows = [*range(REACH), *range(REACH + part, wide)]
    half = cols // 2

    def update(source, dest, row, consts, last):
        for start, count in ((FRONT, half), (FRONT + half, cols - half)):
            dest[row, pl.ds(start, count), :] = advance(source, row, start, count, consts)
        if not last:
            for start, mask in edges:
                value = advance(source, row, start, EDGE, consts)
                dest[row, pl.ds(start, EDGE), :] = jnp.where(mask, value, 0.0)

    buffers = (first, second)

    all_arrived(fine_copies, 0, side_moves)
    def edge_of(start):
        return 0 if start < FRONT else 1

    for start, mask in edges:
        for row in [*range(REACH), *range(part - REACH, part)]:
            raw_edge[edge_of(start), row] = first[row + REACH, pl.ds(start, EDGE), :]
        for row in range(REACH, REACH + part):
            first[row, pl.ds(start, EDGE), :] = jnp.where(mask, first[row, pl.ds(start, EDGE), :], 0.0)
    for step in range(1, SUB + 1):
        def inner_row(row, step=step):
            update(buffers[(step - 1) % 2], buffers[step % 2], row, fine_constants, step == SUB)

        sends_done(fine_copies, 0, y_moves) if step == 2 else None
        pl.loop(REACH + step, REACH + part - step, unroll=2)(inner_row)

    all_arrived(fine_copies, 0, x_moves)
    for row in halo_rows:
        bring_in(row)
        inner = first[row, pl.ds(FRONT, cols), :]
        first[row, pl.ds(FRONT, cols), :] = jnp.where(inside_x(row, REACH, part), inner, 0.0)
    all_arrived(fine_copies, 0, corner_moves)
    for start, mask_y in edges:
        for row in halo_rows:
            here = first[row, pl.ds(start, EDGE), :]
            if row < REACH:
                here = pltpu.roll(jnp.where(high_lanes, here, raw_edge[edge_of(start), row + part - REACH]), levels, 1)
            else:
                here = pltpu.roll(jnp.where(low_lanes, here, raw_edge[edge_of(start), row - part - REACH]), LANES - levels, 1)
            mask = jnp.logical_and(mask_y, inside_x(row, REACH, part))
            first[row, pl.ds(start, EDGE), :] = jnp.where(mask, here, 0.0)
    for step in range(1, SUB + 1):
        def outer_row(row, step=step):
            for shifted in (row, row + part + REACH - 2 * step):
                mask_x = inside_x(shifted, REACH, part)
                consts = tuple(jnp.where(mask_x, c, 0.0) for c in fine_constants)
                update(buffers[(step - 1) % 2], buffers[step % 2], shifted, consts, step == SUB)

        pl.loop(step, REACH + step)(outer_row)
    sends_done(fine_copies, 0, x_moves)
    fine = buffers[SUB % 2]

    for row in range(part_c):
        fine_mean[row] = restricted(fine, row)

    count_c = cols_c + 2 * EDGE
    begin_c = FRONT - EDGE
    mask_y = inside_y(begin_c, count_c, cols_c)

    def extend(buffer, strips):
        _, row_in, _, side_in, _, corner_in = strips
        for side, col in ((0, end_c), (1, FRONT - COARSE_REACH)):
            for row in range(part_c):
                buffer[COARSE_REACH + row, pl.ds(col, COARSE_REACH), :] = side_in[
                    side, pl.ds(COARSE_REACH * row, COARSE_REACH), :
                ]
            for towards in range(2):
                row_in[towards, pl.ds(col, COARSE_REACH), :] = corner_in[towards, side, pl.ds(0, COARSE_REACH), :]

        def own(row):
            return buffer[COARSE_REACH + row, pl.ds(begin_c, count_c), :]

        above, below = (row_in[towards, pl.ds(begin_c, count_c), :] for towards in (0, 1))
        values = [
            jnp.where(low_lanes, below, swapped(own(part_c - 2))),
            swapped(jnp.where(high_lanes, below, own(part_c - 1))),
            *[own(row) for row in range(part_c)],
            swapped(jnp.where(low_lanes, above, own(0))),
            jnp.where(high_lanes, above, swapped(own(1))),
        ]
        for row, value in enumerate(values):
            mask = mask_y
            if not COARSE_REACH <= row < COARSE_REACH + part_c:
                mask = jnp.logical_and(mask_y, inside_x(row, COARSE_REACH, part_c))
            extended[row, pl.ds(begin_c, count_c), :] = jnp.where(mask, value, 0.0)

    all_arrived(old_copies, 0, AROUND)
    sends_done(old_copies, 0, AROUND)
    extend(old_wide, old_strips)
    for row in range(1, wide_c - 1):
        old_image[row - 1] = advance(extended, row, begin_c, count_c, coarse_constants)

    pl.when(tm < n_tm - 1)(lambda: pl.semaphore_wait(ready, 1))

    def write_fine():
        for row in range(part):
            turned[row] = fine[REACH + row, pl.ds(FRONT, cols), :].T

    @pl.when(tm > 0)
    def _():
        write_fine()
        all_arrived(chain_copies, 1, PLANE)
        extend(new_wide, new_strips)

    for row in range(1, wide_c - 1):
        moved = advance(extended, row, begin_c, count_c, coarse_constants) - old_image[row - 1]
        mask = jnp.logical_and(mask_y, inside_x(row, COARSE_REACH, part_c))
        change[row - 1, pl.ds(begin_c, count_c), :] = jnp.where(mask, moved, 0.0)

    def change_row(row):
        return change[row, pl.ds(begin_c, count_c), :]

    @pl.when(tm < n_tm - 1)
    def _():
        for row in range(part_c):
            line[pl.ds(begin_c, count_c), :] = (
                mean_side * (change_row(row) + change_row(row + 2)) + mean_mid * change_row(row + 1)
            )
            sides = line[pl.ds(FRONT - 1, cols_c), :] + line[pl.ds(FRONT + 1, cols_c), :]
            sent[row] = fine_mean[row] + mean_side * sides + mean_mid * line[pl.ds(FRONT, cols_c), :]
        pack_strips(lambda row, col, count: sent[row, pl.ds(col, count), :], new_strips)
        send_all(chain_copies, 1, AROUND)
        send_all(chain_copies, 1, ((0, 0),))

    pl.when(tm == 0)(write_fine)

    coarse_col = lax.broadcasted_iota(jnp.int32, (count_c, cols), 0) - EDGE
    fine_col = lax.broadcasted_iota(jnp.int32, (count_c, cols), 1)
    offset_of = fine_col & (RATIO - 1)
    apart = coarse_col - (fine_col >> (RATIO.bit_length() - 1))
    spreading = jnp.zeros((count_c, cols), jnp.float32)
    for o in range(RATIO):
        for distance, weights in ((-1, weights_low), (0, weights_mid), (1, weights_high)):
            chosen = jnp.logical_and(offset_of == o, apart == distance)
            spreading = jnp.where(chosen, weights[o], spreading)
    spreading = jnp.concatenate([spreading.astype(jnp.bfloat16)] * 3, axis=0)
    for row in range(part_c + 2):
        rest, pieces = change_row(row), []
        for _ in range(3):
            piece = rest.astype(jnp.bfloat16).astype(jnp.float32)
            pieces.append(piece)
            rest = rest - piece
        split = jnp.concatenate(pieces, axis=0).T.astype(jnp.bfloat16)
        spread_rows[row] = jnp.dot(split, spreading, preferred_element_type=jnp.float32)

    for row in range(part):
        at, o = row // RATIO, row % RATIO
        total = turned[row] + weights_mid[o] * spread_rows[at + 1]
        if weights_low[o]:
            total = total + weights_low[o] * spread_rows[at]
        if weights_high[o]:
            total = total + weights_high[o] * spread_rows[at + 2]
        for p in range(packs):
            out_ref[pl.ds(p * part + row, levels, stride=rows), :] = total[p * levels : (p + 1) * levels]

    pl.when(tm < n_tm - 1)(lambda: sends_done(chain_copies, 1, PLANE))


def shards(sizes, state_starts, diffusivity, wind):
    _, levels, rows, cols = state_starts.shape
    packs = LANES // levels
    if packs != 2 or levels * packs != LANES:
        raise ValueError(levels)
    part = rows // packs
    part_c = part // RATIO
    cols_c = cols // RATIO
    wide, wide_c = part + 2 * REACH, part_c + 2 * COARSE_REACH
    vmem = functools.partial(pltpu.VMEM, dtype=jnp.float32)
    scratch = [
        vmem((levels * rows, cols)),
        pltpu.SemaphoreType.DMA,
        pltpu.SemaphoreType.REGULAR,
        vmem((wide, cols + 2 * FRONT, LANES)),
        vmem((wide, cols + 2 * FRONT, LANES)),
        vmem((2, REACH, levels, cols)),
        vmem((2, REACH, levels, cols)),
        vmem((wide_c, cols_c + 2 * FRONT, LANES)),
        vmem((wide_c, cols_c + 2 * FRONT, LANES)),
        vmem((wide_c, cols_c + 2 * FRONT, LANES)),
        vmem((wide_c - 2, cols_c + 2 * EDGE, LANES)),
        vmem((wide_c - 2, cols_c + 2 * FRONT, LANES)),
        vmem((part_c, cols_c, LANES)),
        vmem((part_c, cols_c, LANES)),
        vmem((cols_c + 2 * FRONT, LANES)),
        vmem((cols, LANES)),
        vmem((2, part, EDGE, LANES)),
        vmem((part_c + 2, LANES, cols)),
        vmem((part, LANES, cols)),
    ] + [pltpu.SemaphoreType.DMA((9,))] * 6
    scratch += [
        vmem((2, cols_c, LANES)),
        vmem((2, cols_c + 2 * FRONT, LANES)),
        vmem((2, COARSE_REACH * part_c, LANES)),
        vmem((2, COARSE_REACH * part_c, LANES)),
        vmem((2, 2, EDGE, LANES)),
        vmem((2, 2, EDGE, LANES)),
    ] * 2
    in_vmem = pl.BlockSpec(memory_space=pltpu.VMEM)
    ending = pl.pallas_call(
        functools.partial(kernel, sizes, levels, rows, cols),
        out_shape=pltpu.VMEM((levels * rows, cols), jnp.float32),
        in_specs=[pl.BlockSpec(memory_space=pl.ANY), in_vmem, in_vmem],
        out_specs=in_vmem,
        scratch_shapes=scratch,
        compiler_params=pltpu.CompilerParams(collective_id=0, has_side_effects=True),
        name="parareal",
    )(state_starts.reshape(levels * rows, cols), diffusivity.reshape(1, levels), wind)
    return ending.reshape(1, levels, rows, cols)


def solution(mesh):
    sizes = tuple(mesh.shape[axis] for axis in ("tm", "gx", "gy"))
    placed = (P("tm", None, "gx", "gy"), P(), P())
    return jax.shard_map(
        functools.partial(shards, sizes),
        mesh=mesh, in_specs=placed, out_specs=P("tm", None, "gx", "gy"), check_vma=False,
    )
```
